32 devices in a mesh: pix: 8 (over z, y), ang: 4 (over x, core).
Axes of the slice: x: 2, y: 2, z: 4, core: 2. Of those that a mesh axis runs over, the one named last changes fastest.
Arguments:
- tiles: float32 [8, 4, 512, 4096], P('pix', 'ang'), may hold values from 0.01 to 1
- tile_ray: int32 [8, 4, 512], P('pix', 'ang'), may hold values from 0 to 31, as said below
- tile_pix: int32 [8, 4, 512], P('pix', 'ang'), may hold values from 0 to 7, as said below
- tile_count: int32 [8, 4], P('pix', 'ang'), may hold values from 128 to 512, as said below
- ray_slot: int32 [4, 32], P('ang'), may hold values from 0 to 31, as said below
- image: float32 [4096, 128], P(('pix', 'ang')), may hold values from 0 to 2
- measured: float32 [4, 2048, 128], P('ang', 'pix'), may hold values from -6144 to 6144
Outputs:
- new_image: float32 [4096, 128], P(('pix', 'ang'))
- scaled_resid: float32 [4, 2048, 128], P('ang', 'pix')
The draws below stay inside these ranges and needn't reach their ends.
Inputs may be any that keep to these rules, and one draw needn't show every extreme that they name: Device (p, a) uses only its first tile_count[p, a] tiles; some device uses all 512. `tile_ray`: the used tiles of the devices of one angle group a together name every ray block of that group. `tile_pix`: the used tiles of the devices of one region p together name every pixel block of that region. `ray_slot`: each row is a permutation; slot s lies on the device with pix index s // 4.
All inputs are finite; a program needn't handle non-finite values.
Results may differ from the reference program's by a relative error of at most 0.0003.
Values sent between devices are 32-bit elements; how exact they have to be, the bound alone decides.
No kernel may reach another device: no remote copies, remote signals or barrier semaphores. Data moves between devices by JAX's collectives and lax.ppermute only.
A program may use at most 64 MiB of HBM per device.

```python
import math
import jax
import jax.numpy as jnp
from jax import lax

BLK = 64
S = 128
SLOTS = 512
RBD = 4
PXB_DEV = 2
RB_A = 32
RAYS_A = 2048
PB = 8
NPIX = 4096
N_PIX = 8
N_ANG = 4


def draw_tile_count(key, part):
    first_key, second_key = jax.random.split(jax.random.fold_in(key, 7))
    counts = jax.random.randint(first_key, (N_PIX * N_ANG,), SLOTS // 4, SLOTS + 1)
    busiest = jax.random.randint(second_key, (), 0, N_PIX * N_ANG)
    counts = counts.at[busiest].set(SLOTS)
    return counts.reshape(N_PIX, N_ANG).astype(jnp.int32)


def draw_tile_ray(key, part):
    first_key, second_key = jax.random.split(jax.random.fold_in(key, 11))
    random_rays = jax.random.randint(first_key, (N_PIX, N_ANG, SLOTS), 0, RB_A)
    shifts = jax.random.randint(second_key, (N_PIX, N_ANG, 1), 0, RBD)
    positions = jnp.arange(SLOTS)[None, None, :]
    owners = jnp.arange(N_PIX)[:, None, None]
    covering = owners * RBD + (positions + shifts) % RBD
    return jnp.where(positions < RBD, covering, random_rays).astype(jnp.int32)


def draw_tile_pix(key, part):
    first_key, second_key = jax.random.split(jax.random.fold_in(key, 13))
    random_pixels = jax.random.randint(first_key, (N_PIX, N_ANG, SLOTS), 0, PB)
    shifts = jax.random.randint(second_key, (N_PIX, N_ANG, 1), 0, PXB_DEV)
    positions = jnp.arange(SLOTS)[None, None, :]
    angles = jnp.arange(N_ANG)[None, :, None]
    covering = angles * PXB_DEV + (positions + shifts) % PXB_DEV
    return jnp.where(positions < PXB_DEV, covering, random_pixels).astype(jnp.int32)


def draw_ray_slot(key, part):
    keys = jax.random.split(jax.random.fold_in(key, 17), N_ANG)
    return jax.vmap(lambda single_key: jax.random.permutation(single_key, RB_A))(keys).astype(jnp.int32)


def block_scale(key, dims, shards, low, largest):
    def one(dim, shards_of):
        steps = jax.random.uniform(jax.random.fold_in(jax.random.fold_in(key, 6), dim), (shards_of,), jnp.float32, low / len(shards), largest / len(shards))
        return jnp.repeat(jnp.exp(steps), dims[dim] // shards_of).reshape((-1,) + (1,) * (len(dims) - dim - 1))

    gain = one(*shards[0])
    for cut in shards[1:]:
        gain = gain * one(*cut)
    return gain


def normal_values(rng, shape, deviation, most, cuts=(), kind=jnp.bfloat16):
    array = jax.random.normal(rng, shape, jnp.float32) * deviation
    if len(cuts) > 0:
        array = block_scale(rng, shape, cuts, -0.22, 0.18) * array
    return jnp.clip(array, min=-most, max=most).astype(kind)


def setup_inputs(seed: int = 0) -> dict:
    key_of = jax.random.split(jax.random.key(seed), 8)
    return {
        "tiles": jnp.clip(jnp.exp(math.log(1.0) - 4.6051702 * jax.random.uniform(key_of[0], (N_PIX, N_ANG, SLOTS, BLK * BLK), jnp.float32) ** block_scale(key_of[0], (N_PIX, N_ANG, SLOTS, BLK * BLK), ((0, 8), (1, 4)), -0.2, 0.2)), 0.01, 1.0),
        "tile_ray": draw_tile_ray(jax.random.fold_in(key_of[7], 71), 0),
        "tile_pix": draw_tile_pix(jax.random.fold_in(key_of[7], 71), 0),
        "tile_count": draw_tile_count(jax.random.fold_in(key_of[7], 71), 0),
        "ray_slot": draw_ray_slot(jax.random.fold_in(key_of[7], 71), 0),
        "image": jnp.clip(2.0 * jax.random.uniform(key_of[5], (NPIX, S), jnp.float32) ** block_scale(key_of[5], (NPIX, S), ((0, 32),), -0.2, 0.2), 0.0, 2.0),
        "measured": normal_values(key_of[6], (N_ANG, RAYS_A, S), (SLOTS * BLK // (8 * RBD)), 6144.0, ((0, 4), (1, 8)), jnp.float32),
    }


relax_factor = 0.9


def reference(tiles, tile_ray, tile_pix, tile_count, ray_slot, image, measured):
    group_image = image.reshape(N_PIX, PB, BLK, S)
    positions = jnp.arange(SLOTS, dtype=jnp.int32)

    def device_tiles(device):
        region = device // N_ANG
        angle = device % N_ANG
        active = (positions < tile_count[region, angle]).astype(jnp.float32)
        matrices = tiles[region, angle].reshape(SLOTS, BLK, BLK) * active[:, None, None]
        return region, angle, matrices

    def forward(device, state_tuple):
        proj, row_sums, col_sums = state_tuple
        region, angle, matrices = device_tiles(device)
        pixel_blocks = group_image[region][tile_pix[region, angle]]
        contrib = jnp.einsum("tij,tjs->tis", matrices, pixel_blocks, precision=lax.Precision.HIGHEST)
        proj = proj.at[angle, tile_ray[region, angle]].add(contrib)
        row_sums = row_sums.at[angle, tile_ray[region, angle]].add(jnp.sum(matrices, axis=2))
        col_sums = col_sums.at[region, tile_pix[region, angle]].add(jnp.sum(matrices, axis=1))
        return proj, row_sums, col_sums

    start_state = (jnp.zeros((N_ANG, RB_A, BLK, S), jnp.float32),
                   jnp.zeros((N_ANG, RB_A, BLK), jnp.float32),
                   jnp.zeros((N_PIX, PB, BLK), jnp.float32))
    proj, row_sums, col_sums = lax.fori_loop(0, N_PIX * N_ANG, forward, start_state)
    measured_blocks = measured.reshape(N_ANG, RB_A, BLK, S)
    measured_rays = jnp.take_along_axis(measured_blocks, ray_slot[:, :, None, None], axis=1)
    resid = (measured_rays - proj) / row_sums[..., None]

    def backward(device, back):
        region, angle, matrices = device_tiles(device)
        ray_blocks = resid[angle][tile_ray[region, angle]]
        contrib = jnp.einsum("tij,tis->tjs", matrices, ray_blocks, precision=lax.Precision.HIGHEST)
        return back.at[region, tile_pix[region, angle]].add(contrib)

    back = lax.fori_loop(0, N_PIX * N_ANG, backward, jnp.zeros((N_PIX, PB, BLK, S), jnp.float32))
    new_image = image + relax_factor * (back / col_sums[..., None]).reshape(NPIX, S)
    angles = jnp.arange(N_ANG, dtype=jnp.int32)[:, None]
    slot_resid = jnp.zeros((N_ANG, RB_A, BLK, S), jnp.float32).at[angles, ray_slot].set(resid)
    return new_image, slot_resid.reshape(N_ANG, RAYS_A, S)
```

```python
import functools

import jax
import jax.numpy as jnp
from jax import lax
from jax.experimental import pallas as pl
from jax.experimental.pallas import tpu as pltpu
from jax.sharding import PartitionSpec as P

RELAX = 0.9
F32 = jnp.float32
BF16 = jnp.bfloat16
EXTRA = 8


def split(x):
    high = x.astype(BF16)
    return high, (x - high.astype(F32)).astype(BF16)


def place(rel, order):
    pos = jnp.zeros_like(rel)
    for bit in order:
        pos = pos * 2 + ((rel >> bit) & 1)
    return pos


def orders(size):
    bits = list(range(size.bit_length() - 1))
    return bits, ([bits[1], bits[0]] + bits[2:] if len(bits) > 1 else bits)


def build_kernel(dims, ray_ref, pix_ref, slots_ref, count_ref, x_ref, high_ref, low_ref, hot_ref, dense_ref):
    npix, nang, rays, own, pxd, blk, step = dims
    slots = ray_ref.shape[1]
    pairs = nang * pxd // 2

    @pl.when(pl.program_id(0) == 0)
    def _():
        me, ang = lax.axis_index("pix"), lax.axis_index("ang")
        ray = ray_ref[...]
        slot = jnp.zeros_like(ray)
        for r in range(rays):
            slot = jnp.where(ray == r, slots_ref[0, r], slot)
        inner = slot % own
        half = inner // (own // 2)
        rel = (slot // own) ^ me
        first, second = orders(npix)
        pos = jnp.where(half == 0, place(rel, first), place(rel, second))
        row = half * (rays // 2) + pos * (own // 2) + inner % (own // 2)
        pix = pix_ref[...]
        column = place((pix // pxd) ^ ang, orders(nang)[0]) * pxd + pix % pxd
        block = (column % 2) * (pairs * rays) + (column // 2) * rays + row
        number = lax.broadcasted_iota(jnp.int32, (1, slots), 1)
        block = jnp.where(number < count_ref[0, 0], block, -1)
        rows = lax.broadcasted_iota(jnp.int32, (2 * pairs * rays, slots), 0)
        hot_ref[...] = (rows == block).astype(F32).astype(BF16)

    lanes = 2 * blk
    left = lax.broadcasted_iota(jnp.int32, (pairs * rays, lanes), 1) < blk
    group = 2
    for g in range(step // 2 // group):
        x = x_ref[:, g * group * lanes : (g + 1) * group * lanes]
        high, low = split(x)
        hot = hot_ref[...]
        sums = jnp.dot(hot, high, preferred_element_type=F32) + jnp.dot(hot, low, preferred_element_type=F32)
        for k in range(group):
            c = g * group + k
            even = sums[: pairs * rays, k * lanes : (k + 1) * lanes]
            odd = sums[pairs * rays :, k * lanes : (k + 1) * lanes]
            upper = jnp.where(left, even, pltpu.roll(odd, blk, 1))
            lower = jnp.where(left, pltpu.roll(even, blk, 1), odd)
            for i, value in ((2 * c, upper), (2 * c + 1, lower)):
                for p in range(pairs):
                    dense_ref[pl.ds(p * rays * step + i, rays, stride=step), :] = value[p * rays : (p + 1) * rays]
    for p in range(pairs):
        high, low = split(dense_ref[p * rays * step : (p + 1) * rays * step, :])
        high_ref[:, :, p * lanes : (p + 1) * lanes] = high.reshape(rays, step, lanes)
        low_ref[:, :, p * lanes : (p + 1) * lanes] = low.reshape(rays, step, lanes)


def build(tiles, tile_ray, tile_pix, ray_slot, tile_count, dims):
    npix, nang, rays, own, pxd, blk, step = dims
    slots = tiles.shape[0]
    columns = nang * pxd * blk
    shape = jax.ShapeDtypeStruct((rays, blk, columns), BF16)
    whole = lambda g: (0, 0)
    out = pl.BlockSpec((rays, step, columns), lambda g: (0, g, 0))
    return pl.pallas_call(
        functools.partial(build_kernel, dims),
        grid=(blk // step,),
        in_specs=[
            pl.BlockSpec((1, slots), whole),
            pl.BlockSpec((1, slots), whole),
            pl.BlockSpec(memory_space=pltpu.SMEM),
            pl.BlockSpec(memory_space=pltpu.SMEM),
            pl.BlockSpec((slots, step * blk), lambda g: (0, g)),
        ],
        out_specs=[out, out],
        out_shape=[shape, shape],
        scratch_shapes=[
            pltpu.VMEM((nang * pxd * rays, slots), BF16),
            pltpu.VMEM((nang * pxd // 2 * rays * step, 2 * blk), F32),
        ],
        compiler_params=pltpu.CompilerParams(dimension_semantics=("arbitrary",)),
        cost_estimate=pl.CostEstimate(
            flops=4 * nang * pxd * rays * slots * blk * blk, bytes_accessed=tiles.size * 4 + 4 * rays * blk * columns, transcendentals=0
        ),
        name="build",
    )(tile_ray, tile_pix, ray_slot, tile_count, tiles)


def loop(count, body):
    if count <= 16:
        for k in range(count):
            body(k)
    else:
        lax.fori_loop(0, count, lambda k, c: (body(k), c)[1], 0)


def forward_kernel(image_ref, high_ref, low_ref, out_ref, lhs_ref):
    parts, width, s = image_ref.shape
    for k in range(parts):
        high, low = split(image_ref[k].T)
        lhs_ref[:s, k * width : (k + 1) * width] = high
        lhs_ref[s : 2 * s, k * width : (k + 1) * width] = low
    lhs_ref[2 * s :, :] = jnp.ones((2 * EXTRA, lhs_ref.shape[1]), BF16)
    piece = out_ref.shape[2]
    nt = (((1,), (1,)), ((), ()))

    def body(k):
        rows = pl.ds(k * 2 * piece, 2 * piece)
        lhs = lhs_ref[...]
        r = lax.dot_general(lhs, high_ref[rows, :], nt, preferred_element_type=F32)
        r = r + lax.dot_general(lhs, low_ref[rows, :], nt, preferred_element_type=F32)
        for h in range(2):
            part = r[:, h * piece : (h + 1) * piece]
            out_ref[2 * k + h, :s, :] = part[:s] + part[s : 2 * s]
            out_ref[2 * k + h, s:, :] = part[2 * s : 2 * s + EXTRA]

    loop(out_ref.shape[0] // 2, body)


def forward(image, high, low, piece):
    parts, width, s = image.shape
    rows, columns = high.shape
    vmem = pl.BlockSpec(memory_space=pltpu.VMEM)
    return pl.pallas_call(
        forward_kernel,
        in_specs=[vmem] * 3,
        out_specs=vmem,
        out_shape=jax.ShapeDtypeStruct((rows // piece, s + EXTRA, piece), F32),
        scratch_shapes=[pltpu.VMEM((2 * s + 2 * EXTRA, columns), BF16)],
        cost_estimate=pl.CostEstimate(flops=8 * rows * columns * s, bytes_accessed=4 * rows * columns, transcendentals=0),
        name="forward",
    )(image, high, low)


def backward_kernel(resid_ref, high_ref, low_ref, out_ref, acc_ref):
    s, piece = resid_ref.shape[1:]
    acc_ref[...] = jnp.zeros_like(acc_ref)
    ones = jnp.ones((2 * EXTRA, 2 * piece), BF16)

    def body(k):
        high, low = split(jnp.concatenate([resid_ref[2 * k], resid_ref[2 * k + 1]], axis=1))
        lhs = jnp.concatenate([high, low, ones], axis=0)
        rows = pl.ds(k * 2 * piece, 2 * piece)
        acc_ref[...] += jnp.dot(lhs, high_ref[rows, :], preferred_element_type=F32) + jnp.dot(
            lhs, low_ref[rows, :], preferred_element_type=F32
        )

    loop(resid_ref.shape[0] // 2, body)
    width = out_ref.shape[2]
    for p in range(out_ref.shape[0]):
        part = acc_ref[:, p * width : (p + 1) * width]
        out_ref[p, :s, :] = part[:s] + part[s : 2 * s]
        out_ref[p, s:, :] = part[2 * s : 2 * s + EXTRA]


def backward(resid, high, low, parts):
    pieces, s, piece = resid.shape
    rows, columns = high.shape
    vmem = pl.BlockSpec(memory_space=pltpu.VMEM)
    return pl.pallas_call(
        backward_kernel,
        in_specs=[vmem] * 3,
        out_specs=vmem,
        out_shape=jax.ShapeDtypeStruct((parts, s + EXTRA, columns // parts), F32),
        scratch_shapes=[pltpu.VMEM((2 * s + 2 * EXTRA, columns), F32)],
        cost_estimate=pl.CostEstimate(flops=8 * rows * columns * s, bytes_accessed=4 * rows * columns, transcendentals=0),
        name="backward",
    )(resid, high, low)


def swap(x, axis, bit):
    size = lax.axis_size(axis)
    return lax.ppermute(x, axis, [(i, i ^ (1 << bit)) for i in range(size)])


def shards(tiles, tile_ray, tile_pix, tile_count, ray_slot, image, measured):
    npix, nang = lax.axis_size("pix"), lax.axis_size("ang")
    rays, slots = ray_slot.shape[1], tiles.shape[2]
    own = rays // npix
    blk = measured.shape[1] // own
    s = image.shape[1]
    pxd = image.shape[0] // blk
    dims = (npix, nang, rays, own, pxd, blk, 16)
    piece = own * blk // 2
    first, second = orders(npix)
    steps = len(first)

    gathered = image[None]
    for bit in reversed(orders(nang)[0]):
        gathered = jnp.concatenate([gathered, swap(gathered, "ang", bit)])
    high, low = build(tiles.reshape(slots, blk * blk), tile_ray[0], tile_pix[0], ray_slot, tile_count, dims)
    columns = high.shape[2]
    high, low = high.reshape(rays * blk, columns), low.reshape(rays * blk, columns)

    proj = forward(gathered, high, low, piece).reshape(2, npix, s + EXTRA, piece)
    a, b = proj[0], proj[1]
    for t in range(min(2, steps)):
        m = a.shape[0] // 2
        a, b = a[:m] + swap(a[m:], "pix", first[t]), b[:m] + swap(b[m:], "pix", second[t])
    both = jnp.stack([a, b])
    for t in range(2, steps):
        m = both.shape[1] // 2
        both = both[:, :m] + swap(both[:, m:], "pix", first[t])
    total = both[:, 0]
    wanted = jnp.swapaxes(measured[0].reshape(2, piece, s), 1, 2)
    resid = (wanted - total[:, :s]) / total[:, s : s + 1]
    resid_own = jnp.swapaxes(resid, 1, 2).reshape(1, 2 * piece, s)

    both = resid[:, None]
    for t in reversed(range(2, steps)):
        both = jnp.concatenate([both, swap(both, "pix", first[t])], axis=1)
    a, b = both[0], both[1]
    for t in reversed(range(min(2, steps))):
        a, b = (
            jnp.concatenate([a, swap(a, "pix", first[t])]),
            jnp.concatenate([b, swap(b, "pix", second[t])]),
        )
    back = backward(jnp.concatenate([a, b]), high, low, nang)
    for bit in orders(nang)[0]:
        m = back.shape[0] // 2
        back = back[:m] + swap(back[m:], "ang", bit)
    back = back[0]
    new_image = image + RELAX * (back[:s] / back[s : s + 1]).T
    return new_image, resid_own


def solution(mesh):
    in_specs = (
        P("pix", "ang", None, None),
        P("pix", "ang", None),
        P("pix", "ang", None),
        P("pix", "ang"),
        P("ang", None),
        P(("pix", "ang"), None),
        P("ang", "pix", None),
    )
    out_specs = (P(("pix", "ang"), None), P("ang", "pix", None))
    return jax.shard_map(shards, mesh=mesh, in_specs=in_specs, out_specs=out_specs, check_vma=False)
```

```python
import functools

import jax
import jax.numpy as jnp
import numpy as np
from jax import lax
from jax.experimental import pallas as pl
from jax.experimental.pallas import tpu as pltpu
from jax.sharding import PartitionSpec as P

RELAX = 0.9
F32 = jnp.float32
BF16 = jnp.bfloat16
EXTRA = 8


def split(x):
    high = x.astype(BF16)
    return high, (x - high.astype(F32)).astype(BF16)


def place(rel, order):
    pos = rel * 0
    for bit in order:
        pos = pos * 2 + ((rel >> bit) & 1)
    return pos


def orders(size):
    bits = list(range(size.bit_length() - 1))
    return bits, ([bits[1], bits[0]] + bits[2:] if len(bits) > 1 else bits)


def build_kernel(dims, ray_ref, pix_ref, slots_ref, count_ref, x_ref, high_ref, low_ref, hot_ref, dense_ref):
    npix, nang, rays, own, pxd, blk, step = dims
    slots = ray_ref.shape[1]
    pairs = nang * pxd // 2

    @pl.when(pl.program_id(0) == 0)
    def _():
        me, ang = lax.axis_index("pix"), lax.axis_index("ang")
        ray = ray_ref[...]
        slot = jnp.zeros_like(ray)
        for r in range(rays):
            slot = jnp.where(ray == r, slots_ref[0, r], slot)
        inner = slot % own
        half = inner // (own // 2)
        rel = (slot // own) ^ me
        first, second = orders(npix)
        pos = jnp.where(half == 0, place(rel, first), place(rel, second))
        row = half * (rays // 2) + pos * (own // 2) + inner % (own // 2)
        pix = pix_ref[...]
        column = place((pix // pxd) ^ ang, orders(nang)[0]) * pxd + pix % pxd
        block = (column % 2) * (pairs * rays) + (column // 2) * rays + row
        number = lax.broadcasted_iota(jnp.int32, (1, slots), 1)
        block = jnp.where(number < count_ref[0, 0], block, -1)
        rows = lax.broadcasted_iota(jnp.int32, (2 * pairs * rays, slots), 0)
        hot_ref[...] = (rows == block).astype(F32).astype(BF16)

    lanes = 2 * blk
    left = lax.broadcasted_iota(jnp.int32, (pairs * rays, lanes), 1) < blk
    group = 2
    for g in range(step // 2 // group):
        x = x_ref[:, g * group * lanes : (g + 1) * group * lanes]
        high, low = split(x)
        hot = hot_ref[...]
        sums = jnp.dot(hot, high, preferred_element_type=F32) + jnp.dot(hot, low, preferred_element_type=F32)
        for k in range(group):
            c = g * group + k
            even = sums[: pairs * rays, k * lanes : (k + 1) * lanes]
            odd = sums[pairs * rays :, k * lanes : (k + 1) * lanes]
            upper = jnp.where(left, even, pltpu.roll(odd, blk, 1))
            lower = jnp.where(left, pltpu.roll(even, blk, 1), odd)
            for i, value in ((2 * c, upper), (2 * c + 1, lower)):
                for p in range(pairs):
                    dense_ref[pl.ds(p * rays * step + i, rays, stride=step), :] = value[p * rays : (p + 1) * rays]
    for p in range(pairs):
        high, low = split(dense_ref[p * rays * step : (p + 1) * rays * step, :])
        high_ref[:, :, p * lanes : (p + 1) * lanes] = high.reshape(rays, step, lanes)
        low_ref[:, :, p * lanes : (p + 1) * lanes] = low.reshape(rays, step, lanes)


def build(tiles, tile_ray, tile_pix, ray_slot, tile_count, dims):
    npix, nang, rays, own, pxd, blk, step = dims
    slots = tiles.shape[0]
    columns = nang * pxd * blk
    shape = jax.ShapeDtypeStruct((rays, blk, columns), BF16)
    whole = lambda g: (0, 0)
    out = pl.BlockSpec((rays, step, columns), lambda g: (0, g, 0))
    return pl.pallas_call(
        functools.partial(build_kernel, dims),
        grid=(blk // step,),
        in_specs=[
            pl.BlockSpec((1, slots), whole),
            pl.BlockSpec((1, slots), whole),
            pl.BlockSpec(memory_space=pltpu.SMEM),
            pl.BlockSpec(memory_space=pltpu.SMEM),
            pl.BlockSpec((slots, step * blk), lambda g: (0, g)),
        ],
        out_specs=[out, out],
        out_shape=[shape, shape],
        scratch_shapes=[
            pltpu.VMEM((nang * pxd * rays, slots), BF16),
            pltpu.VMEM((nang * pxd // 2 * rays * step, 2 * blk), F32),
        ],
        compiler_params=pltpu.CompilerParams(
            dimension_semantics=("arbitrary",), vmem_limit_bytes=min(60 << 20, 20 * rays * step * columns + 8 * tiles.size * step // blk + (8 << 20))
        ),
        cost_estimate=pl.CostEstimate(
            flops=4 * nang * pxd * rays * slots * blk * blk, bytes_accessed=tiles.size * 4 + 4 * rays * blk * columns, transcendentals=0
        ),
        name="build",
    )(tile_ray, tile_pix, ray_slot, tile_count, tiles)


def loop(count, body):
    if count <= 16:
        for k in range(count):
            body(k)
    else:
        lax.fori_loop(0, count, lambda k, c: (body(k), c)[1], 0)


def size_of(*shapes):
    total = 0
    for x in shapes:
        count = 1
        for d in x.shape:
            count *= d
        total += count * jnp.dtype(x.dtype).itemsize
    return total


def limit(*shapes):
    return min(size_of(*shapes) + (6 << 20), 60 << 20)


VMEM = pl.BlockSpec(memory_space=pltpu.VMEM)
NT = (((1,), (1,)), ((), ()))


def project(lhs_ref, high_ref, low_ref, out_ref, start):
    pieces, tall, piece = out_ref.shape
    s = tall - EXTRA

    def body(k):
        rows = pl.ds(start + k * 2 * piece, 2 * piece)
        lhs = lhs_ref[...]
        r = lax.dot_general(lhs, high_ref[rows, :], NT, preferred_element_type=F32)
        r = r + lax.dot_general(lhs, low_ref[rows, :], NT, preferred_element_type=F32)
        for h in range(2):
            part = r[:, h * piece : (h + 1) * piece]
            out_ref[2 * k + h, :s, :] = part[:s] + part[s : 2 * s]
            out_ref[2 * k + h, s:, :] = part[2 * s : 2 * s + EXTRA]

    loop(pieces // 2, body)


def forward_sent_kernel(parts, *refs):
    images, (high_ref, low_ref, a_ref, b_ref, lhs_ref) = refs[: len(parts)], refs[len(parts) :]
    for places, image_ref in zip(parts, images, strict=True):
        for k, place_of in enumerate(places):
            width, s = image_ref.shape[1:]
            high, low = split(image_ref[k].T)
            lhs_ref[:s, place_of * width : (place_of + 1) * width] = high
            lhs_ref[s : 2 * s, place_of * width : (place_of + 1) * width] = low
    lhs_ref[2 * s :, :] = jnp.ones((2 * EXTRA, lhs_ref.shape[1]), BF16)
    half = high_ref.shape[0] // 2
    project(lhs_ref, high_ref, low_ref, a_ref, half // 2)
    project(lhs_ref, high_ref, low_ref, b_ref, half + half // 2)


def forward_kept_kernel(lhs_ref, high_ref, low_ref, a_ref, b_ref):
    project(lhs_ref, high_ref, low_ref, a_ref, 0)
    project(lhs_ref, high_ref, low_ref, b_ref, high_ref.shape[0] // 2)


def forward(images, parts, high, low, piece):
    s = images[0].shape[2]
    rows, columns = high.shape
    out = jax.ShapeDtypeStruct((rows // piece // 4, s + EXTRA, piece), F32)
    lhs = jax.ShapeDtypeStruct((2 * s + 2 * EXTRA, columns), BF16)
    cost = pl.CostEstimate(flops=4 * rows * columns * s, bytes_accessed=2 * rows * columns, transcendentals=0)
    params = pltpu.CompilerParams(vmem_limit_bytes=limit(high, low, out, out, lhs, *images))
    a_sent, b_sent, lhs = pl.pallas_call(
        functools.partial(forward_sent_kernel, parts),
        in_specs=[VMEM] * (2 + len(images)),
        out_specs=[VMEM] * 3,
        out_shape=[out, out, lhs],
        cost_estimate=cost,
        compiler_params=params,
        name="forward_sent",
    )(*images, high, low)
    a_kept, b_kept = pl.pallas_call(
        forward_kept_kernel,
        in_specs=[VMEM] * 3,
        out_specs=[VMEM] * 2,
        out_shape=[out, out],
        cost_estimate=cost,
        compiler_params=params,
        name="forward_kept",
    )(lhs, high, low)
    return a_kept, a_sent, b_kept, b_sent


def spread(resid_ref, high_ref, low_ref, start, total):
    pieces, s, piece = resid_ref.shape
    ones = jnp.ones((2 * EXTRA, 2 * piece), BF16)

    def body(k):
        high, low = split(jnp.concatenate([resid_ref[2 * k], resid_ref[2 * k + 1]], axis=1))
        lhs = jnp.concatenate([high, low, ones], axis=0)
        rows = pl.ds(start + k * 2 * piece, 2 * piece)
        total[...] += jnp.dot(lhs, high_ref[rows, :], preferred_element_type=F32) + jnp.dot(
            lhs, low_ref[rows, :], preferred_element_type=F32
        )

    loop(pieces // 2, body)


def backward_held_kernel(a_ref, b_ref, high_ref, low_ref, total_ref):
    total_ref[...] = jnp.zeros_like(total_ref)
    spread(a_ref, high_ref, low_ref, 0, total_ref)
    spread(b_ref, high_ref, low_ref, high_ref.shape[0] // 2, total_ref)


def backward_got_kernel(a_ref, b_ref, high_ref, low_ref, before_ref, kept_ref, sent_ref, total_ref):
    total_ref[...] = before_ref[...]
    half = high_ref.shape[0] // 2
    spread(a_ref, high_ref, low_ref, half // 2, total_ref)
    spread(b_ref, high_ref, low_ref, half + half // 2, total_ref)
    pieces, tall, width = kept_ref.shape
    s = tall - EXTRA
    for p in range(2 * pieces):
        out_ref, k = (kept_ref, p) if p < pieces else (sent_ref, p - pieces)
        part = total_ref[:, p * width : (p + 1) * width]
        out_ref[k, :s, :] = part[:s] + part[s : 2 * s]
        out_ref[k, s:, :] = part[2 * s : 2 * s + EXTRA]


def backward(a_held, a_got, b_held, b_got, high, low, parts):
    s = a_held.shape[1]
    rows, columns = high.shape
    total = jax.ShapeDtypeStruct((2 * s + 2 * EXTRA, columns), F32)
    out = jax.ShapeDtypeStruct((parts // 2, s + EXTRA, columns // parts), F32)
    cost = pl.CostEstimate(flops=4 * rows * columns * s, bytes_accessed=2 * rows * columns, transcendentals=0)
    params = pltpu.CompilerParams(vmem_limit_bytes=limit(high, low, total, total, out, out, a_held, b_held))
    total = pl.pallas_call(
        backward_held_kernel,
        in_specs=[VMEM] * 4,
        out_specs=VMEM,
        out_shape=total,
        cost_estimate=cost,
        compiler_params=params,
        name="backward_held",
    )(a_held, b_held, high, low)
    return pl.pallas_call(
        backward_got_kernel,
        in_specs=[VMEM] * 5,
        out_specs=[VMEM] * 2,
        out_shape=[out, out],
        scratch_shapes=[pltpu.VMEM(total.shape, F32)],
        cost_estimate=cost,
        compiler_params=params,
        name="backward_got",
    )(a_got, b_got, high, low, total)


def swap(x, axis, bit):
    size = lax.axis_size(axis)
    return lax.ppermute(x, axis, [(i, i ^ (1 << bit)) for i in range(size)])


def shards(tiles, tile_ray, tile_pix, tile_count, ray_slot, image, measured):
    npix, nang = lax.axis_size("pix"), lax.axis_size("ang")
    rays, slots = ray_slot.shape[1], tiles.shape[2]
    own = rays // npix
    blk = measured.shape[1] // own
    s = image.shape[1]
    pxd = image.shape[0] // blk
    dims = (npix, nang, rays, own, pxd, blk, 16)
    piece = own * blk // 2
    first, second = orders(npix)
    steps = len(first)

    images, rels = [image[None]], [[0]]
    for bit in range(nang.bit_length() - 1):
        images.append(swap(jnp.concatenate(images), "ang", bit))
        rels.append([r ^ (1 << bit) for group in rels for r in group])
    parts = [[int(place(np.int32(r), orders(nang)[0])) for r in group] for group in rels]
    high, low = build(tiles.reshape(slots, blk * blk), tile_ray[0], tile_pix[0], ray_slot, tile_count, dims)
    columns = high.shape[2]
    high, low = high.reshape(rays * blk, columns), low.reshape(rays * blk, columns)

    a_kept, a_sent, b_kept, b_sent = forward(images, parts, high, low, piece)
    for t in range(2):
        a_got, b_got = swap(a_sent, "pix", first[t]), swap(b_sent, "pix", second[t])
        m = a_kept.shape[0] // 2
        a_kept, a_sent = a_kept[:m] + a_got[:m], a_kept[m:] + a_got[m:]
        b_kept, b_sent = b_kept[:m] + b_got[:m], b_kept[m:] + b_got[m:]
    kept, sent = jnp.stack([a_kept, b_kept]), jnp.stack([a_sent, b_sent])
    for t in range(2, steps):
        got = swap(sent, "pix", first[t])
        m = kept.shape[1] // 2
        kept, sent = (kept[:, :m] + got[:, :m], kept[:, m:] + got[:, m:]) if m else (kept + got, None)
    total = kept[:, 0]
    wanted = jnp.swapaxes(measured[0].reshape(2, piece, s), 1, 2)
    resid = (wanted - total[:, :s]) / total[:, s : s + 1]
    resid_own = jnp.swapaxes(resid, 1, 2).reshape(1, 2 * piece, s)

    both = resid[:, None]
    for t in reversed(range(2, steps)):
        both = jnp.concatenate([both, swap(both, "pix", first[t])], axis=1)
    a, b = both[0], both[1]
    a, b = (
        jnp.concatenate([a, swap(a, "pix", first[1])]),
        jnp.concatenate([b, swap(b, "pix", second[1])]),
    )
    a_got, b_got = swap(a, "pix", first[0]), swap(b, "pix", second[0])
    kept, sent = backward(a, a_got, b, b_got, high, low, nang)
    for bit in orders(nang)[0]:
        got = swap(sent, "ang", bit)
        m = kept.shape[0] // 2
        kept, sent = (kept[:m] + got[:m], kept[m:] + got[m:]) if m else (kept + got, None)
    back = kept[0]
    new_image = image + RELAX * (back[:s] / back[s : s + 1]).T
    return new_image, resid_own


def solution(mesh):
    in_specs = (
        P("pix", "ang", None, None),
        P("pix", "ang", None),
        P("pix", "ang", None),
        P("pix", "ang"),
        P("ang", None),
        P(("pix", "ang"), None),
        P("ang", "pix", None),
    )
    out_specs = (P(("pix", "ang"), None), P("ang", "pix", None))
    return jax.shard_map(shards, mesh=mesh, in_specs=in_specs, out_specs=out_specs, check_vma=False)
```

```python
import functools

import jax
import jax.numpy as jnp
import numpy as np
from jax import lax
from jax.experimental import pallas as pl
from jax.experimental.pallas import tpu as pltpu
from jax.sharding import PartitionSpec as P

RELAX = 0.9
F32 = jnp.float32
BF16 = jnp.bfloat16
EXTRA = 8


def split(x):
    high = x.astype(BF16)
    return high, (x - high.astype(F32)).astype(BF16)


def place(rel, order):
    pos = rel * 0
    for bit in order:
        pos = pos * 2 + ((rel >> bit) & 1)
    return pos


def orders(size):
    bits = list(range(size.bit_length() - 1))
    return bits, ([bits[1], bits[0]] + bits[2:] if len(bits) > 1 else bits)


def size_of(*shapes):
    total = 0
    for x in shapes:
        count = 1
        for d in x.shape:
            count *= d
        total += count * jnp.dtype(x.dtype).itemsize
    return total


def limit(*shapes):
    return min(size_of(*shapes) + (6 << 20), 60 << 20)


VMEM = pl.BlockSpec(memory_space=pltpu.VMEM)


def build_kernel(dims, x_hbm, ray_hbm, pix_hbm, slots_hbm, count_hbm, high_ref, low_ref, *scratch):
    npix, nang, rays, own, pxd, blk, step = dims
    x_ref, ray_ref, pix_ref, slots_ref, count_ref, hot_ref, dense_ref, small_sem, x_sem = scratch
    slots = ray_ref.shape[1]
    pairs = nang * pxd // 2
    lanes = 2 * blk
    small = [
        pltpu.make_async_copy(source, target, small_sem.at[k])
        for k, (source, target) in enumerate(
            ((ray_hbm, ray_ref), (pix_hbm, pix_ref), (slots_hbm, slots_ref), (count_hbm, count_ref))
        )
    ]
    width = step * blk
    large = [
        pltpu.make_async_copy(x_hbm.at[:, pl.ds(k * width, width)], x_ref.at[:, pl.ds(k * width, width)], x_sem.at[k])
        for k in range(blk // step)
    ]
    for copy in small + large:
        copy.start()
    for copy in small:
        copy.wait()

    me, ang = lax.axis_index("pix"), lax.axis_index("ang")
    ray = ray_ref[...]
    slot = jnp.zeros_like(ray)
    for r in range(rays):
        slot = jnp.where(ray == r, slots_ref[0, r], slot)
    inner = slot % own
    half = inner // (own // 2)
    rel = (slot // own) ^ me
    first, second = orders(npix)
    pos = jnp.where(half == 0, place(rel, first), place(rel, second))
    row = half * (rays // 2) + pos * (own // 2) + inner % (own // 2)
    pix = pix_ref[...]
    column = place((pix // pxd) ^ ang, orders(nang)[0]) * pxd + pix % pxd
    block = (column % 2) * (pairs * rays) + (column // 2) * rays + row
    number = lax.broadcasted_iota(jnp.int32, (1, slots), 1)
    block = jnp.where(number < count_ref[0, 0], block, -1)
    rows = lax.broadcasted_iota(jnp.int32, (2 * pairs * rays, slots), 0)
    hot_ref[...] = (rows == block).astype(F32).astype(BF16)

    left = lax.broadcasted_iota(jnp.int32, (pairs * rays, lanes), 1) < blk
    group = 2
    for n in range(blk // step):
        large[n].wait()
        for g in range(step // 2 // group):
            start = n * width + g * group * lanes
            high, low = split(x_ref[:, start : start + group * lanes])
            hot = hot_ref[...]
            sums = jnp.dot(hot, high, preferred_element_type=F32) + jnp.dot(hot, low, preferred_element_type=F32)
            for k in range(group):
                c = g * group + k
                even = sums[: pairs * rays, k * lanes : (k + 1) * lanes]
                odd = sums[pairs * rays :, k * lanes : (k + 1) * lanes]
                upper = jnp.where(left, even, pltpu.roll(odd, blk, 1))
                lower = jnp.where(left, pltpu.roll(even, blk, 1), odd)
                for i, value in ((2 * c, upper), (2 * c + 1, lower)):
                    for p in range(pairs):
                        dense_ref[pl.ds(p * rays * step + i, rays, stride=step), :] = value[p * rays : (p + 1) * rays]
        for p in range(pairs):
            high, low = split(dense_ref[p * rays * step : (p + 1) * rays * step, :])
            at = (slice(None), slice(n * step, (n + 1) * step), slice(p * lanes, (p + 1) * lanes))
            high_ref[at] = high.reshape(rays, step, lanes)
            low_ref[at] = low.reshape(rays, step, lanes)


def build(tiles, tile_ray, tile_pix, ray_slot, tile_count, dims):
    npix, nang, rays, own, pxd, blk, step = dims
    slots = tiles.shape[0]
    columns = nang * pxd * blk
    shape = jax.ShapeDtypeStruct((rays, blk, columns), BF16)
    hot = jax.ShapeDtypeStruct((nang * pxd * rays, slots), BF16)
    dense = jax.ShapeDtypeStruct((nang * pxd // 2 * rays * step, 2 * blk), F32)
    hbm = pl.BlockSpec(memory_space=pltpu.HBM)
    small = size_of(shape, shape) <= 6 << 20
    grant = 58 << 20 if small else limit(tiles, shape, shape, hot, dense)
    return pl.pallas_call(
        functools.partial(build_kernel, dims),
        in_specs=[hbm] * 5,
        out_specs=[VMEM] * 2,
        out_shape=[pltpu.VMEM(shape.shape, BF16) if small else shape] * 2,
        scratch_shapes=[
            pltpu.VMEM(tiles.shape, F32),
            pltpu.VMEM(tile_ray.shape, jnp.int32),
            pltpu.VMEM(tile_pix.shape, jnp.int32),
            pltpu.SMEM(ray_slot.shape, jnp.int32),
            pltpu.SMEM(tile_count.shape, jnp.int32),
            pltpu.VMEM(hot.shape, BF16),
            pltpu.VMEM(dense.shape, F32),
            pltpu.SemaphoreType.DMA((4,)),
            pltpu.SemaphoreType.DMA((blk // step,)),
        ],
        compiler_params=pltpu.CompilerParams(vmem_limit_bytes=grant),
        cost_estimate=pl.CostEstimate(
            flops=4 * nang * pxd * rays * slots * blk * blk, bytes_accessed=tiles.size * 4 + 4 * rays * blk * columns, transcendentals=0
        ),
        name="build",
    )(tiles, tile_ray, tile_pix, ray_slot, tile_count)


def loop(count, body):
    if count <= 16:
        for k in range(count):
            body(k)
    else:
        lax.fori_loop(0, count, lambda k, c: (body(k), c)[1], 0)


NT = (((1,), (1,)), ((), ()))


def project(lhs_ref, high_ref, low_ref, out_ref, start):
    pieces, tall, piece = out_ref.shape
    s = tall - EXTRA

    def body(k):
        rows = pl.ds(start + k * 2 * piece, 2 * piece)
        lhs = lhs_ref[...]
        r = lax.dot_general(lhs, high_ref[rows, :], NT, preferred_element_type=F32)
        r = r + lax.dot_general(lhs, low_ref[rows, :], NT, preferred_element_type=F32)
        for h in range(2):
            part = r[:, h * piece : (h + 1) * piece]
            out_ref[2 * k + h, :s, :] = part[:s] + part[s : 2 * s]
            out_ref[2 * k + h, s:, :] = part[2 * s : 2 * s + EXTRA]

    loop(pieces // 2, body)


def forward_sent_kernel(parts, *refs):
    images, (high_ref, low_ref, a_ref, b_ref, lhs_ref) = refs[: len(parts)], refs[len(parts) :]
    for places, image_ref in zip(parts, images, strict=True):
        for k, place_of in enumerate(places):
            width, s = image_ref.shape[1:]
            high, low = split(image_ref[k].T)
            lhs_ref[:s, place_of * width : (place_of + 1) * width] = high
            lhs_ref[s : 2 * s, place_of * width : (place_of + 1) * width] = low
    lhs_ref[2 * s :, :] = jnp.ones((2 * EXTRA, lhs_ref.shape[1]), BF16)
    half = high_ref.shape[0] // 2
    project(lhs_ref, high_ref, low_ref, a_ref, half // 2)
    project(lhs_ref, high_ref, low_ref, b_ref, half + half // 2)


def forward_kept_kernel(lhs_ref, high_ref, low_ref, a_ref, b_ref):
    project(lhs_ref, high_ref, low_ref, a_ref, 0)
    project(lhs_ref, high_ref, low_ref, b_ref, high_ref.shape[0] // 2)


def forward(images, parts, high, low, piece):
    s = images[0].shape[2]
    rows, columns = high.shape
    out = jax.ShapeDtypeStruct((rows // piece // 4, s + EXTRA, piece), F32)
    lhs = jax.ShapeDtypeStruct((2 * s + 2 * EXTRA, columns), BF16)
    cost = pl.CostEstimate(flops=4 * rows * columns * s, bytes_accessed=2 * rows * columns, transcendentals=0)
    params = pltpu.CompilerParams(vmem_limit_bytes=limit(high, low, out, out, lhs, *images))
    a_sent, b_sent, lhs = pl.pallas_call(
        functools.partial(forward_sent_kernel, parts),
        in_specs=[VMEM] * (2 + len(images)),
        out_specs=[VMEM] * 3,
        out_shape=[out, out, lhs],
        cost_estimate=cost,
        compiler_params=params,
        name="forward_sent",
    )(*images, high, low)
    a_kept, b_kept = pl.pallas_call(
        forward_kept_kernel,
        in_specs=[VMEM] * 3,
        out_specs=[VMEM] * 2,
        out_shape=[out, out],
        cost_estimate=cost,
        compiler_params=params,
        name="forward_kept",
    )(lhs, high, low)
    return a_kept, a_sent, b_kept, b_sent


def spread(resid_ref, high_ref, low_ref, start, total):
    pieces, s, piece = resid_ref.shape
    ones = jnp.ones((2 * EXTRA, 2 * piece), BF16)

    def body(k):
        high, low = split(jnp.concatenate([resid_ref[2 * k], resid_ref[2 * k + 1]], axis=1))
        lhs = jnp.concatenate([high, low, ones], axis=0)
        rows = pl.ds(start + k * 2 * piece, 2 * piece)
        total[...] += jnp.dot(lhs, high_ref[rows, :], preferred_element_type=F32) + jnp.dot(
            lhs, low_ref[rows, :], preferred_element_type=F32
        )

    loop(pieces // 2, body)


def backward_held_kernel(a_ref, b_ref, high_ref, low_ref, total_ref):
    total_ref[...] = jnp.zeros_like(total_ref)
    spread(a_ref, high_ref, low_ref, 0, total_ref)
    spread(b_ref, high_ref, low_ref, high_ref.shape[0] // 2, total_ref)


def backward_got_kernel(a_ref, b_ref, high_ref, low_ref, before_ref, kept_ref, sent_ref, total_ref):
    total_ref[...] = before_ref[...]
    half = high_ref.shape[0] // 2
    spread(a_ref, high_ref, low_ref, half // 2, total_ref)
    spread(b_ref, high_ref, low_ref, half + half // 2, total_ref)
    pieces, tall, width = kept_ref.shape
    s = tall - EXTRA
    for p in range(2 * pieces):
        out_ref, k = (kept_ref, p) if p < pieces else (sent_ref, p - pieces)
        part = total_ref[:, p * width : (p + 1) * width]
        out_ref[k, :s, :] = part[:s] + part[s : 2 * s]
        out_ref[k, s:, :] = part[2 * s : 2 * s + EXTRA]


def backward(a_held, a_got, b_held, b_got, high, low, parts):
    s = a_held.shape[1]
    rows, columns = high.shape
    total = jax.ShapeDtypeStruct((2 * s + 2 * EXTRA, columns), F32)
    out = jax.ShapeDtypeStruct((parts // 2, s + EXTRA, columns // parts), F32)
    cost = pl.CostEstimate(flops=4 * rows * columns * s, bytes_accessed=2 * rows * columns, transcendentals=0)
    params = pltpu.CompilerParams(vmem_limit_bytes=limit(high, low, total, total, out, out, a_held, b_held))
    total = pl.pallas_call(
        backward_held_kernel,
        in_specs=[VMEM] * 4,
        out_specs=VMEM,
        out_shape=total,
        cost_estimate=cost,
        compiler_params=params,
        name="backward_held",
    )(a_held, b_held, high, low)
    return pl.pallas_call(
        backward_got_kernel,
        in_specs=[VMEM] * 5,
        out_specs=[VMEM] * 2,
        out_shape=[out, out],
        scratch_shapes=[pltpu.VMEM(total.shape, F32)],
        cost_estimate=cost,
        compiler_params=params,
        name="backward_got",
    )(a_got, b_got, high, low, total)


def swap(x, axis, mask):
    size = lax.axis_size(axis)
    return lax.ppermute(x, axis, [(i, i ^ mask) for i in range(size)])


def shards(tiles, tile_ray, tile_pix, tile_count, ray_slot, image, measured):
    npix, nang = lax.axis_size("pix"), lax.axis_size("ang")
    rays, slots = ray_slot.shape[1], tiles.shape[2]
    own = rays // npix
    blk = measured.shape[1] // own
    s = image.shape[1]
    pxd = image.shape[0] // blk
    dims = (npix, nang, rays, own, pxd, blk, 16)
    piece = own * blk // 2
    first, second = orders(npix)
    steps = len(first)

    images, rels = [image[None]] + [swap(image[None], "ang", r) for r in range(1, nang)], range(nang)
    high, low = build(tiles.reshape(slots, blk * blk), tile_ray[0], tile_pix[0], ray_slot, tile_count, dims)
    parts = [[int(place(np.int32(r), orders(nang)[0]))] for r in rels]
    columns = high.shape[2]
    high, low = high.reshape(rays * blk, columns), low.reshape(rays * blk, columns)

    a_kept, a_sent, b_kept, b_sent = forward(images, parts, high, low, piece)
    for t in range(2):
        a_got, b_got = swap(a_sent, "pix", 1 << first[t]), swap(b_sent, "pix", 1 << second[t])
        m = a_kept.shape[0] // 2
        a_kept, a_sent = a_kept[:m] + a_got[:m], a_kept[m:] + a_got[m:]
        b_kept, b_sent = b_kept[:m] + b_got[:m], b_kept[m:] + b_got[m:]
    kept, sent = jnp.stack([a_kept, b_kept]), jnp.stack([a_sent, b_sent])
    for t in range(2, steps):
        got = swap(sent, "pix", 1 << first[t])
        m = kept.shape[1] // 2
        kept, sent = (kept[:, :m] + got[:, :m], kept[:, m:] + got[:, m:]) if m else (kept + got, None)
    total = kept[:, 0]
    wanted = jnp.swapaxes(measured[0].reshape(2, piece, s), 1, 2)
    resid = (wanted - total[:, :s]) / total[:, s : s + 1]
    resid_own = jnp.swapaxes(resid, 1, 2).reshape(1, 2 * piece, s)

    both = resid[:, None]
    for t in reversed(range(2, steps)):
        both = jnp.concatenate([both, swap(both, "pix", 1 << first[t])], axis=1)
    a, b = both[0], both[1]
    a, b = (
        jnp.concatenate([a, swap(a, "pix", 1 << first[1])]),
        jnp.concatenate([b, swap(b, "pix", 1 << second[1])]),
    )
    a_got, b_got = swap(a, "pix", 1 << first[0]), swap(b, "pix", 1 << second[0])
    kept, sent = backward(a, a_got, b, b_got, high, low, nang)
    for bit in orders(nang)[0]:
        got = swap(sent, "ang", 1 << bit)
        m = kept.shape[0] // 2
        kept, sent = (kept[:m] + got[:m], kept[m:] + got[m:]) if m else (kept + got, None)
    back = kept[0]
    new_image = image + RELAX * (back[:s] / back[s : s + 1]).T
    return new_image, resid_own


def solution(mesh):
    in_specs = (
        P("pix", "ang", None, None),
        P("pix", "ang", None),
        P("pix", "ang", None),
        P("pix", "ang"),
        P("ang", None),
        P(("pix", "ang"), None),
        P("ang", "pix", None),
    )
    out_specs = (P(("pix", "ang"), None), P("ang", "pix", None))
    return jax.shard_map(shards, mesh=mesh, in_specs=in_specs, out_specs=out_specs, check_vma=False)
```

```python
import functools

import jax
import jax.numpy as jnp
import numpy as np
from jax import lax
from jax.experimental import pallas as pl
from jax.experimental.pallas import tpu as pltpu
from jax.sharding import PartitionSpec as P

RELAX = 0.9
F32 = jnp.float32
BF16 = jnp.bfloat16
EXTRA = 8


def split(x):
    high = x.astype(BF16)
    return high, (x - high.astype(F32)).astype(BF16)


def place(rel, order):
    pos = rel * 0
    for bit in order:
        pos = pos * 2 + ((rel >> bit) & 1)
    return pos


def bits_of(size):
    return list(range(size.bit_length() - 1))


def size_of(*shapes):
    total = 0
    for x in shapes:
        count = 1
        for d in x.shape:
            count *= d
        total += count * jnp.dtype(x.dtype).itemsize
    return total


def limit(*shapes):
    return min(size_of(*shapes) + (6 << 20), 60 << 20)


VMEM = pl.BlockSpec(memory_space=pltpu.VMEM)


def build_kernel(dims, x_hbm, ray_hbm, pix_hbm, slots_hbm, count_hbm, high_ref, low_ref, *scratch):
    npix, nang, rays, own, pxd, blk, step = dims
    x_ref, ray_ref, pix_ref, slots_ref, count_ref, hot_ref, dense_ref, small_sem, x_sem = scratch
    slots = ray_ref.shape[1]
    pairs = nang * pxd // 2
    lanes = 2 * blk
    small = [
        pltpu.make_async_copy(source, target, small_sem.at[k])
        for k, (source, target) in enumerate(
            ((ray_hbm, ray_ref), (pix_hbm, pix_ref), (slots_hbm, slots_ref), (count_hbm, count_ref))
        )
    ]
    width = step * blk
    large = [
        pltpu.make_async_copy(x_hbm.at[:, pl.ds(k * width, width)], x_ref.at[:, pl.ds(k * width, width)], x_sem.at[k])
        for k in range(blk // step)
    ]
    for copy in small + large:
        copy.start()
    for copy in small:
        copy.wait()

    me, ang = lax.axis_index("pix"), lax.axis_index("ang")
    ray = ray_ref[...]
    slot = jnp.zeros_like(ray)
    for r in range(rays):
        slot = jnp.where(ray == r, slots_ref[0, r], slot)
    rel = (slot // own) ^ me
    pos = (rel % 8) * (npix // 8) + rel // 8
    row = pos * own + slot % own
    pix = pix_ref[...]
    column = place((pix // pxd) ^ ang, bits_of(nang)) * pxd + pix % pxd
    block = (column % 2) * (pairs * rays) + (column // 2) * rays + row
    number = lax.broadcasted_iota(jnp.int32, (1, slots), 1)
    block = jnp.where(number < count_ref[0, 0], block, -1)
    rows = lax.broadcasted_iota(jnp.int32, (2 * pairs * rays, slots), 0)
    hot_ref[...] = (rows == block).astype(F32).astype(BF16)

    left = lax.broadcasted_iota(jnp.int32, (pairs * rays, lanes), 1) < blk
    group = 2
    for n in range(blk // step):
        large[n].wait()
        for g in range(step // 2 // group):
            start = n * width + g * group * lanes
            high, low = split(x_ref[:, start : start + group * lanes])
            hot = hot_ref[...]
            sums = jnp.dot(hot, high, preferred_element_type=F32) + jnp.dot(hot, low, preferred_element_type=F32)
            for k in range(group):
                c = g * group + k
                even = sums[: pairs * rays, k * lanes : (k + 1) * lanes]
                odd = sums[pairs * rays :, k * lanes : (k + 1) * lanes]
                upper = jnp.where(left, even, pltpu.roll(odd, blk, 1))
                lower = jnp.where(left, pltpu.roll(even, blk, 1), odd)
                for i, value in ((2 * c, upper), (2 * c + 1, lower)):
                    for p in range(pairs):
                        dense_ref[pl.ds(p * rays * step + i, rays, stride=step), :] = value[p * rays : (p + 1) * rays]
        for p in range(pairs):
            high, low = split(dense_ref[p * rays * step : (p + 1) * rays * step, :])
            at = (slice(None), slice(n * step, (n + 1) * step), slice(p * lanes, (p + 1) * lanes))
            high_ref[at] = high.reshape(rays, step, lanes)
            low_ref[at] = low.reshape(rays, step, lanes)


def build(tiles, tile_ray, tile_pix, ray_slot, tile_count, dims):
    npix, nang, rays, own, pxd, blk, step = dims
    slots = tiles.shape[0]
    columns = nang * pxd * blk
    shape = jax.ShapeDtypeStruct((rays, blk, columns), BF16)
    hot = jax.ShapeDtypeStruct((nang * pxd * rays, slots), BF16)
    dense = jax.ShapeDtypeStruct((nang * pxd // 2 * rays * step, 2 * blk), F32)
    hbm = pl.BlockSpec(memory_space=pltpu.HBM)
    small = size_of(shape, shape) <= 6 << 20
    grant = 58 << 20 if small else limit(tiles, shape, shape, hot, dense)
    return pl.pallas_call(
        functools.partial(build_kernel, dims),
        in_specs=[hbm] * 5,
        out_specs=[VMEM] * 2,
        out_shape=[pltpu.VMEM(shape.shape, BF16) if small else shape] * 2,
        scratch_shapes=[
            pltpu.VMEM(tiles.shape, F32),
            pltpu.VMEM(tile_ray.shape, jnp.int32),
            pltpu.VMEM(tile_pix.shape, jnp.int32),
            pltpu.SMEM(ray_slot.shape, jnp.int32),
            pltpu.SMEM(tile_count.shape, jnp.int32),
            pltpu.VMEM(hot.shape, BF16),
            pltpu.VMEM(dense.shape, F32),
            pltpu.SemaphoreType.DMA((4,)),
            pltpu.SemaphoreType.DMA((blk // step,)),
        ],
        compiler_params=pltpu.CompilerParams(vmem_limit_bytes=grant),
        cost_estimate=pl.CostEstimate(
            flops=4 * nang * pxd * rays * slots * blk * blk, bytes_accessed=tiles.size * 4 + 4 * rays * blk * columns, transcendentals=0
        ),
        name="build",
    )(tiles, tile_ray, tile_pix, ray_slot, tile_count)


def loop(count, body):
    if count <= 16:
        for k in range(count):
            body(k)
    else:
        lax.fori_loop(0, count, lambda k, c: (body(k), c)[1], 0)


NT = (((1,), (1,)), ((), ()))


def project(lhs_ref, high_ref, low_ref, out_ref, start):
    pieces, tall, piece = out_ref.shape
    s = tall - EXTRA

    def body(k):
        rows = pl.ds(start + k * piece, piece)
        lhs = lhs_ref[...]
        r = lax.dot_general(lhs, high_ref[rows, :], NT, preferred_element_type=F32)
        r = r + lax.dot_general(lhs, low_ref[rows, :], NT, preferred_element_type=F32)
        out_ref[k, :s, :] = r[:s] + r[s : 2 * s]
        out_ref[k, s:, :] = r[2 * s : 2 * s + EXTRA]

    loop(pieces, body)


def forward_first_kernel(parts, groups, *refs):
    images, (high_ref, low_ref, *outs, lhs_ref) = refs[: len(parts)], refs[len(parts) :]
    for place_of, image_ref in zip(parts, images, strict=True):
        width, s = image_ref.shape
        high, low = split(image_ref[...].T)
        lhs_ref[:s, place_of * width : (place_of + 1) * width] = high
        lhs_ref[s : 2 * s, place_of * width : (place_of + 1) * width] = low
    lhs_ref[2 * s :, :] = jnp.ones((2 * EXTRA, lhs_ref.shape[1]), BF16)
    for g, out_ref in zip(groups, outs, strict=True):
        project(lhs_ref, high_ref, low_ref, out_ref, g * (high_ref.shape[0] // 8))


def forward_rest_kernel(groups, lhs_ref, high_ref, low_ref, *outs):
    for g, out_ref in zip(groups, outs, strict=True):
        project(lhs_ref, high_ref, low_ref, out_ref, g * (high_ref.shape[0] // 8))


def forward(images, parts, high, low, piece, first, rest):
    s = images[0].shape[1]
    rows, columns = high.shape
    out = jax.ShapeDtypeStruct((rows // piece // 8, s + EXTRA, piece), F32)
    lhs = jax.ShapeDtypeStruct((2 * s + 2 * EXTRA, columns), BF16)
    params = pltpu.CompilerParams(vmem_limit_bytes=limit(high, low, lhs, *images, *[out] * len(rest)))

    def cost(groups):
        return pl.CostEstimate(
            flops=len(groups) * rows * columns * s, bytes_accessed=len(groups) * rows * columns // 2, transcendentals=0
        )

    *early, lhs = pl.pallas_call(
        functools.partial(forward_first_kernel, parts, first),
        in_specs=[VMEM] * (2 + len(images)),
        out_specs=[VMEM] * (len(first) + 1),
        out_shape=[out] * len(first) + [lhs],
        cost_estimate=cost(first),
        compiler_params=params,
        name="forward_first",
    )(*images, high, low)
    late = pl.pallas_call(
        functools.partial(forward_rest_kernel, rest),
        in_specs=[VMEM] * 3,
        out_specs=[VMEM] * len(rest),
        out_shape=[out] * len(rest),
        cost_estimate=cost(rest),
        compiler_params=params,
        name="forward_rest",
    )(lhs, high, low)
    return dict(zip([*first, *rest], [*early, *late], strict=True))


def spread(resid_ref, high_ref, low_ref, start, total):
    pieces, s, piece = resid_ref.shape
    ones = jnp.ones((2 * EXTRA, piece), BF16)

    def body(k):
        lhs = jnp.concatenate([*split(resid_ref[k]), ones], axis=0)
        rows = pl.ds(start + k * piece, piece)
        total[...] += jnp.dot(lhs, high_ref[rows, :], preferred_element_type=F32) + jnp.dot(
            lhs, low_ref[rows, :], preferred_element_type=F32
        )

    loop(pieces, body)


def backward_kernel(groups, first, last, *refs):
    resids, (high_ref, low_ref, *rest) = refs[: len(groups)], refs[len(groups) :]
    total = rest[-1]
    total[...] = jnp.zeros_like(total) if first else rest[0][...]
    for g, resid_ref in zip(groups, resids, strict=True):
        spread(resid_ref, high_ref, low_ref, g * (high_ref.shape[0] // 8), total)
    if last:
        kept_ref, sent_ref = rest[-3:-1]
        pieces, tall, width = kept_ref.shape
        s = tall - EXTRA
        for p in range(2 * pieces):
            out_ref, k = (kept_ref, p) if p < pieces else (sent_ref, p - pieces)
            part = total[:, p * width : (p + 1) * width]
            out_ref[k, :s, :] = part[:s] + part[s : 2 * s]
            out_ref[k, s:, :] = part[2 * s : 2 * s + EXTRA]


def backward(resids, high, low, parts, before, last):
    s = next(iter(resids.values())).shape[1]
    rows, columns = high.shape
    total = jax.ShapeDtypeStruct((2 * s + 2 * EXTRA, columns), F32)
    out = jax.ShapeDtypeStruct((parts // 2, s + EXTRA, columns // parts), F32)
    operands = [*resids.values(), high, low] + ([] if before is None else [before])
    return pl.pallas_call(
        functools.partial(backward_kernel, list(resids), before is None, last),
        in_specs=[VMEM] * len(operands),
        out_specs=[VMEM] * 2 if last else VMEM,
        out_shape=[out, out] if last else total,
        scratch_shapes=[pltpu.VMEM(total.shape, F32)] if last else [],
        cost_estimate=pl.CostEstimate(
            flops=len(resids) * rows * columns * s, bytes_accessed=len(resids) * rows * columns // 2, transcendentals=0
        ),
        compiler_params=pltpu.CompilerParams(vmem_limit_bytes=limit(total, total, *operands)),
        name="backward",
    )(*operands)


def swap(x, axis, mask, name):
    with jax.named_scope(name):
        return lax.ppermute(x, axis, [(i, i ^ mask) for i in range(lax.axis_size(axis))])


def shards(tiles, tile_ray, tile_pix, tile_count, ray_slot, image, measured):
    npix, nang = lax.axis_size("pix"), lax.axis_size("ang")
    rays, slots = ray_slot.shape[1], tiles.shape[2]
    own = rays // npix
    blk = measured.shape[1] // own
    s = image.shape[1]
    pxd = image.shape[0] // blk
    dims = (npix, nang, rays, own, pxd, blk, 16)
    piece = own * blk
    more = bits_of(npix)[3:]

    images = [image] + [swap(image, "ang", r, f"image{r}") for r in range(1, nang)]
    high, low = build(tiles.reshape(slots, blk * blk), tile_ray[0], tile_pix[0], ray_slot, tile_count, dims)
    parts = [int(place(np.int32(r), bits_of(nang))) for r in range(nang)]
    columns = high.shape[2]
    high, low = high.reshape(rays * blk, columns), low.reshape(rays * blk, columns)

    proj = forward(images, parts, high, low, piece, [7, 5, 6], [1, 2, 3, 4, 0])
    far = [swap(proj[4 + d], "pix", d, f"far{d}") for d in (3, 1, 2)]
    crossing = swap(proj[4] + far[0] + far[1] + far[2], "pix", 4, "cross")
    near = [swap(proj[d], "pix", d, f"near{d}") for d in (1, 2, 3)]
    total = proj[0] + near[0] + near[1] + near[2] + crossing
    for bit in reversed(more):
        m = total.shape[0] // 2
        total = total[:m] + swap(total[m:], "pix", 1 << bit, f"sum{bit}")
    total = total[0]
    resid = (measured[0].T - total[:s]) / total[s : s + 1]
    resid_own = resid.T[None]

    held = resid[None]
    for bit in more:
        held = jnp.concatenate([held, swap(held, "pix", 1 << bit, f"give{bit}")])
    got = {0: held, 4: swap(held, "pix", 4, "recross")}
    for d in (1, 3, 2):
        got[d] = swap(held, "pix", d, f"renear{d}")
    for d in (3, 1, 2):
        got[4 + d] = swap(got[4], "pix", d, f"refar{d}")
    back = backward({g: got[g] for g in (0, 1, 2, 3)}, high, low, nang, None, False)
    back = backward({g: got[g] for g in (4, 7)}, high, low, nang, back, False)
    kept, sent = backward({g: got[g] for g in (5, 6)}, high, low, nang, back, True)
    for bit in bits_of(nang):
        arrived = swap(sent, "ang", 1 << bit, f"back{bit}")
        m = kept.shape[0] // 2
        kept, sent = (kept[:m] + arrived[:m], kept[m:] + arrived[m:]) if m else (kept + arrived, None)
    back = kept[0]
    new_image = image + RELAX * (back[:s] / back[s : s + 1]).T
    return new_image, resid_own


def solution(mesh):
    in_specs = (
        P("pix", "ang", None, None),
        P("pix", "ang", None),
        P("pix", "ang", None),
        P("pix", "ang"),
        P("ang", None),
        P(("pix", "ang"), None),
        P("ang", "pix", None),
    )
    out_specs = (P(("pix", "ang"), None), P("ang", "pix", None))
    return jax.shard_map(shards, mesh=mesh, in_specs=in_specs, out_specs=out_specs, check_vma=False)
```

```python
import functools

import jax
import jax.numpy as jnp
import numpy as np
from jax import lax
from jax.experimental import pallas as pl
from jax.experimental.pallas import tpu as pltpu
from jax.sharding import PartitionSpec as P

RELAX = 0.9
F32 = jnp.float32
BF16 = jnp.bfloat16
EXTRA = 8


def split(x):
    high = x.astype(BF16)
    return high, (x - high.astype(F32)).astype(BF16)


def place(rel, order):
    pos = rel * 0
    for bit in order:
        pos = pos * 2 + ((rel >> bit) & 1)
    return pos


def bits_of(size):
    return list(range(size.bit_length() - 1))


def size_of(*shapes):
    total = 0
    for x in shapes:
        count = 1
        for d in x.shape:
            count *= d
        total += count * jnp.dtype(x.dtype).itemsize
    return total


def limit(*shapes):
    return min(size_of(*shapes) + (6 << 20), 60 << 20)


VMEM = pl.BlockSpec(memory_space=pltpu.VMEM)


def build_kernel(dims, x_hbm, ray_hbm, pix_hbm, slots_hbm, count_hbm, out_ref, *scratch):
    npix, nang, rays, own, pxd, blk, step = dims
    x_ref, ray_ref, pix_ref, slots_ref, count_ref, hot_ref, small_sem, x_sem = scratch
    slots = ray_ref.shape[1]
    pairs = nang * pxd // 2
    lanes = 2 * blk
    small = [
        pltpu.make_async_copy(source, target, small_sem.at[k])
        for k, (source, target) in enumerate(
            ((ray_hbm, ray_ref), (pix_hbm, pix_ref), (slots_hbm, slots_ref), (count_hbm, count_ref))
        )
    ]
    width = step * blk
    large = [
        pltpu.make_async_copy(x_hbm.at[:, pl.ds(k * width, width)], x_ref.at[:, pl.ds(k * width, width)], x_sem.at[k])
        for k in range(blk // step)
    ]
    for copy in small + large:
        copy.start()
    for copy in small:
        copy.wait()

    me, ang = lax.axis_index("pix"), lax.axis_index("ang")
    ray = ray_ref[...]
    slot = jnp.zeros_like(ray)
    for r in range(rays):
        slot = jnp.where(ray == r, slots_ref[0, r], slot)
    rel = (slot // own) ^ me
    pos = (rel % 8) * (npix // 8) + rel // 8
    row = pos * own + slot % own
    pix = pix_ref[...]
    column = place((pix // pxd) ^ ang, bits_of(nang)) * pxd + pix % pxd
    block = (column // 2) * (2 * rays) + (column % 2) * rays + row
    number = lax.broadcasted_iota(jnp.int32, (1, slots), 1)
    block = jnp.where(number < count_ref[0, 0], block, -1)
    rows = lax.broadcasted_iota(jnp.int32, (2 * pairs * rays, slots), 0)
    hot_ref[...] = (rows == block).astype(F32).astype(BF16)

    pack = rays // 8
    left = lax.broadcasted_iota(jnp.int32, (rays, lanes), 1) < blk
    above = lax.broadcasted_iota(jnp.int32, (pack, 8, lanes), 1) < 4

    def rows_of(sums, p, k):
        even = sums[2 * p * rays : (2 * p + 1) * rays, k * lanes : (k + 1) * lanes]
        odd = sums[(2 * p + 1) * rays : (2 * p + 2) * rays, k * lanes : (k + 1) * lanes]
        upper = jnp.where(left, even, pltpu.roll(odd, blk, 1)).reshape(pack, 8, lanes)
        lower = jnp.where(left, pltpu.roll(even, blk, 1), odd).reshape(pack, 8, lanes)
        return jnp.where(above, upper, pltpu.roll(lower, 4, 1)), jnp.where(above, pltpu.roll(upper, 4, 1), lower)

    for n in range(blk // step):
        large[n].wait()
        for g in range(step // 4):
            start = n * width + g * 2 * lanes
            high, low = split(x_ref[:, start : start + 2 * lanes])
            hot = hot_ref[...]
            sums = jnp.dot(hot, high, preferred_element_type=F32) + jnp.dot(hot, low, preferred_element_type=F32)
            at = 16 * (n * step // 4 + g)
            for p in range(pairs):
                for owner, value in enumerate(zip(rows_of(sums, p, 0), rows_of(sums, p, 1), strict=True)):
                    high, low = split(jnp.concatenate(value, axis=1))
                    out_ref[:, owner, at : at + 16, p * lanes : (p + 1) * lanes] = high
                    out_ref[:, owner, at : at + 16, (pairs + p) * lanes : (pairs + p + 1) * lanes] = low


def build(tiles, tile_ray, tile_pix, ray_slot, tile_count, dims):
    npix, nang, rays, own, pxd, blk, step = dims
    slots = tiles.shape[0]
    assert own == 4 and npix % 8 == 0 and pxd == 2
    columns = nang * pxd * blk
    shape = jax.ShapeDtypeStruct((npix // 2, 2, own * blk, 2 * columns), BF16)
    hot = jax.ShapeDtypeStruct((nang * pxd * rays, slots), BF16)
    hbm = pl.BlockSpec(memory_space=pltpu.HBM)
    small = size_of(shape) <= 6 << 20
    grant = 58 << 20 if small else limit(tiles, shape, hot)
    return pl.pallas_call(
        functools.partial(build_kernel, dims),
        in_specs=[hbm] * 5,
        out_specs=VMEM,
        out_shape=pltpu.VMEM(shape.shape, BF16) if small else shape,
        scratch_shapes=[
            pltpu.VMEM(tiles.shape, F32),
            pltpu.VMEM(tile_ray.shape, jnp.int32),
            pltpu.VMEM(tile_pix.shape, jnp.int32),
            pltpu.SMEM(ray_slot.shape, jnp.int32),
            pltpu.SMEM(tile_count.shape, jnp.int32),
            pltpu.VMEM(hot.shape, BF16),
            pltpu.SemaphoreType.DMA((4,)),
            pltpu.SemaphoreType.DMA((blk // step,)),
        ],
        compiler_params=pltpu.CompilerParams(vmem_limit_bytes=grant),
        cost_estimate=pl.CostEstimate(
            flops=4 * nang * pxd * rays * slots * blk * blk, bytes_accessed=tiles.size * 4 + 4 * rays * blk * columns, transcendentals=0
        ),
        name="build",
    )(tiles, tile_ray, tile_pix, ray_slot, tile_count).reshape(rays * blk, 2 * columns)


def loop(count, body):
    if count <= 16:
        for k in range(count):
            body(k)
    else:
        lax.fori_loop(0, count, lambda k, c: (body(k), c)[1], 0)


NT = (((1,), (1,)), ((), ()))


def project(lhs_ref, dense_ref, out_ref, start):
    pieces, tall, piece = out_ref.shape
    s = tall - EXTRA

    def body(k):
        rows = pl.ds(start + k * piece, piece)
        r = lax.dot_general(lhs_ref[...], dense_ref[rows, :], NT, preferred_element_type=F32)
        out_ref[k, :s, :] = r[:s] + r[s : 2 * s]
        out_ref[k, s:, :] = r[2 * s : 2 * s + EXTRA]

    loop(pieces, body)


def forward_first_kernel(parts, groups, *refs):
    images, (dense_ref, *outs, lhs_ref) = refs[: len(parts)], refs[len(parts) :]
    columns = lhs_ref.shape[1] // 2
    for place_of, image_ref in zip(parts, images, strict=True):
        width, s = image_ref.shape
        high, low = split(image_ref[...].T)
        for at in (place_of * width, columns + place_of * width):
            lhs_ref[:s, at : at + width] = high
            lhs_ref[s : 2 * s, at : at + width] = low
    lhs_ref[2 * s :, :] = jnp.ones((2 * EXTRA, lhs_ref.shape[1]), BF16)
    for g, out_ref in zip(groups, outs, strict=True):
        project(lhs_ref, dense_ref, out_ref, g * (dense_ref.shape[0] // 8))


def forward_rest_kernel(groups, lhs_ref, dense_ref, *outs):
    for g, out_ref in zip(groups, outs, strict=True):
        project(lhs_ref, dense_ref, out_ref, g * (dense_ref.shape[0] // 8))


def forward(images, parts, dense, piece, first, rest):
    s = images[0].shape[1]
    rows, columns = dense.shape
    out = jax.ShapeDtypeStruct((rows // piece // 8, s + EXTRA, piece), F32)
    lhs = jax.ShapeDtypeStruct((2 * s + 2 * EXTRA, columns), BF16)
    params = pltpu.CompilerParams(vmem_limit_bytes=limit(dense, lhs, *images, *[out] * len(rest)))

    def cost(groups):
        return pl.CostEstimate(
            flops=len(groups) * rows * columns * s // 2, bytes_accessed=len(groups) * rows * columns // 4, transcendentals=0
        )

    *early, lhs = pl.pallas_call(
        functools.partial(forward_first_kernel, parts, first),
        in_specs=[VMEM] * (1 + len(images)),
        out_specs=[VMEM] * (len(first) + 1),
        out_shape=[out] * len(first) + [lhs],
        cost_estimate=cost(first),
        compiler_params=params,
        name="forward_first",
    )(*images, dense)
    late = pl.pallas_call(
        functools.partial(forward_rest_kernel, rest),
        in_specs=[VMEM] * 2,
        out_specs=[VMEM] * len(rest),
        out_shape=[out] * len(rest),
        cost_estimate=cost(rest),
        compiler_params=params,
        name="forward_rest",
    )(lhs, dense)
    return dict(zip([*first, *rest], [*early, *late], strict=True))


def spread(resid_ref, dense_ref, start, total):
    pieces, s, piece = resid_ref.shape
    columns = total.shape[1]
    ones = jnp.ones((2 * EXTRA, piece), BF16)

    def body(k):
        lhs = jnp.concatenate([*split(resid_ref[k]), ones], axis=0)
        rows = pl.ds(start + k * piece, piece)
        both = jnp.concatenate([dense_ref[rows, :columns], dense_ref[rows, columns:]], axis=0)
        total[...] += jnp.dot(jnp.concatenate([lhs, lhs], axis=1), both, preferred_element_type=F32)

    loop(pieces, body)


def backward_kernel(groups, first, last, *refs):
    resids, (dense_ref, *rest) = refs[: len(groups)], refs[len(groups) :]
    total = rest[-1]
    total[...] = jnp.zeros_like(total) if first else rest[0][...]
    for g, resid_ref in zip(groups, resids, strict=True):
        spread(resid_ref, dense_ref, g * (dense_ref.shape[0] // 8), total)
    if last:
        kept_ref, sent_ref = rest[-3:-1]
        pieces, tall, width = kept_ref.shape
        s = tall - EXTRA
        for p in range(2 * pieces):
            out_ref, k = (kept_ref, p) if p < pieces else (sent_ref, p - pieces)
            part = total[:, p * width : (p + 1) * width]
            out_ref[k, :s, :] = part[:s] + part[s : 2 * s]
            out_ref[k, s:, :] = part[2 * s : 2 * s + EXTRA]


def backward(resids, dense, parts, before, last):
    s = next(iter(resids.values())).shape[1]
    rows, columns = dense.shape[0], dense.shape[1] // 2
    total = jax.ShapeDtypeStruct((2 * s + 2 * EXTRA, columns), F32)
    out = jax.ShapeDtypeStruct((parts // 2, s + EXTRA, columns // parts), F32)
    operands = [*resids.values(), dense] + ([] if before is None else [before])
    return pl.pallas_call(
        functools.partial(backward_kernel, list(resids), before is None, last),
        in_specs=[VMEM] * len(operands),
        out_specs=[VMEM] * 2 if last else VMEM,
        out_shape=[out, out] if last else total,
        scratch_shapes=[pltpu.VMEM(total.shape, F32)] if last else [],
        cost_estimate=pl.CostEstimate(
            flops=len(resids) * rows * columns * s, bytes_accessed=len(resids) * rows * columns // 2, transcendentals=0
        ),
        compiler_params=pltpu.CompilerParams(vmem_limit_bytes=limit(total, total, *operands)),
        name="backward",
    )(*operands)


def prepare_kernel(own, measured_ref, out_ref, rows_ref):
    blk = measured_ref.shape[0] // own
    for r in range(own):
        rows_ref[pl.ds(r, blk, stride=own), :] = measured_ref[r * blk : (r + 1) * blk, :]
    out_ref[...] = rows_ref[...].T


def restore_kernel(own, resid_ref, out_ref, rows_ref):
    blk = out_ref.shape[0] // own
    rows_ref[...] = resid_ref[...].T
    for r in range(own):
        out_ref[r * blk : (r + 1) * blk, :] = rows_ref[pl.ds(r, blk, stride=own), :]


def turn(kernel, own, x, name):
    rows = max(x.shape), min(x.shape)
    return pl.pallas_call(
        functools.partial(kernel, own),
        in_specs=[VMEM],
        out_specs=VMEM,
        out_shape=jax.ShapeDtypeStruct(x.shape[::-1], F32),
        scratch_shapes=[pltpu.VMEM(rows, F32)],
        compiler_params=pltpu.CompilerParams(vmem_limit_bytes=limit(x, x)),
        cost_estimate=pl.CostEstimate(flops=x.size, bytes_accessed=8 * x.size, transcendentals=0),
        name=name,
    )(x)


def swap(x, axis, mask, name):
    with jax.named_scope(name):
        return lax.ppermute(x, axis, [(i, i ^ mask) for i in range(lax.axis_size(axis))])


def shards(tiles, tile_ray, tile_pix, tile_count, ray_slot, image, measured):
    npix, nang = lax.axis_size("pix"), lax.axis_size("ang")
    rays, slots = ray_slot.shape[1], tiles.shape[2]
    own = rays // npix
    blk = measured.shape[1] // own
    s = image.shape[1]
    pxd = image.shape[0] // blk
    dims = (npix, nang, rays, own, pxd, blk, 16)
    piece = own * blk
    more = bits_of(npix)[3:]

    images = [image] + [swap(image, "ang", r, f"image{r}") for r in range(1, nang)]
    dense = build(tiles.reshape(slots, blk * blk), tile_ray[0], tile_pix[0], ray_slot, tile_count, dims)
    parts = [int(place(np.int32(r), bits_of(nang))) for r in range(nang)]

    proj = forward(images, parts, dense, piece, [7, 5, 6], [1, 2, 3, 4, 0])
    far = [swap(proj[4 + d], "pix", d, f"far{d}") for d in (2, 1, 3)]
    crossing = swap(proj[4] + far[0] + far[1] + far[2], "pix", 4, "cross")
    near = [swap(proj[d], "pix", d, f"near{d}") for d in (1, 2, 3)]
    total = proj[0] + near[0] + near[1] + near[2] + crossing
    for bit in reversed(more):
        m = total.shape[0] // 2
        total = total[:m] + swap(total[m:], "pix", 1 << bit, f"sum{bit}")
    total = total[0]
    wanted = turn(prepare_kernel, own, measured[0], "prepare")
    resid = (wanted - total[:s]) / total[s : s + 1]
    resid_own = turn(restore_kernel, own, resid, "restore")[None]

    held = resid[None]
    for bit in more:
        held = jnp.concatenate([held, swap(held, "pix", 1 << bit, f"give{bit}")])
    got = {0: held, 4: swap(held, "pix", 4, "recross")}
    for d in (1, 2, 3):
        got[d] = swap(held, "pix", d, f"renear{d}")
    for d in (2, 1, 3):
        got[4 + d] = swap(got[4], "pix", d, f"refar{d}")
    back = backward({g: got[g] for g in (0, 1, 2, 3)}, dense, nang, None, False)
    back = backward({g: got[g] for g in (4, 7)}, dense, nang, back, False)
    kept, sent = backward({g: got[g] for g in (5, 6)}, dense, nang, back, True)
    for bit in bits_of(nang):
        arrived = swap(sent, "ang", 1 << bit, f"back{bit}")
        m = kept.shape[0] // 2
        kept, sent = (kept[:m] + arrived[:m], kept[m:] + arrived[m:]) if m else (kept + arrived, None)
    back = kept[0]
    new_image = image + RELAX * (back[:s] / back[s : s + 1]).T
    return new_image, resid_own


def solution(mesh):
    in_specs = (
        P("pix", "ang", None, None),
        P("pix", "ang", None),
        P("pix", "ang", None),
        P("pix", "ang"),
        P("ang", None),
        P(("pix", "ang"), None),
        P("ang", "pix", None),
    )
    out_specs = (P(("pix", "ang"), None), P("ang", "pix", None))
    return jax.shard_map(shards, mesh=mesh, in_specs=in_specs, out_specs=out_specs, check_vma=False)
```

```python
import functools

import jax
import jax.numpy as jnp
import numpy as np
from jax import lax
from jax.experimental import pallas as pl
from jax.experimental.pallas import tpu as pltpu
from jax.sharding import PartitionSpec as P


RELAX = 0.9
F32 = jnp.float32
BF16 = jnp.bfloat16
EXTRA = 8


def split(x):
    high = x.astype(BF16)
    return high, (x - high.astype(F32)).astype(BF16)


def place(rel, order):
    pos = rel * 0
    for bit in order:
        pos = pos * 2 + ((rel >> bit) & 1)
    return pos


def bits_of(size):
    return list(range(size.bit_length() - 1))


def size_of(*shapes):
    total = 0
    for x in shapes:
        count = 1
        for d in x.shape:
            count *= d
        total += count * jnp.dtype(x.dtype).itemsize
    return total


def limit(*shapes):
    return min(size_of(*shapes) + (6 << 20), 60 << 20)


VMEM = pl.BlockSpec(memory_space=pltpu.VMEM)


def build_kernel(dims, x_hbm, ray_hbm, pix_hbm, slots_hbm, count_hbm, out_ref, *scratch):
    npix, nang, rays, own, pxd, blk, step = dims
    x_ref, ray_ref, pix_ref, slots_ref, count_ref, hot_ref, small_sem, x_sem = scratch
    slots = ray_ref.shape[1]
    pairs = nang * pxd // 2
    lanes = 2 * blk
    small = [
        pltpu.make_async_copy(source, target, small_sem.at[k])
        for k, (source, target) in enumerate(
            ((ray_hbm, ray_ref), (pix_hbm, pix_ref), (slots_hbm, slots_ref), (count_hbm, count_ref))
        )
    ]
    width = step * blk
    large = [
        pltpu.make_async_copy(x_hbm.at[:, pl.ds(k * width, width)], x_ref.at[:, pl.ds(k * width, width)], x_sem.at[k])
        for k in range(blk // step)
    ]
    for copy in small + large:
        copy.start()
    for copy in small:
        copy.wait()

    me, ang = lax.axis_index("pix"), lax.axis_index("ang")
    ray = ray_ref[...]
    slot = jnp.zeros_like(ray)
    for r in range(rays):
        slot = jnp.where(ray == r, slots_ref[0, r], slot)
    rel = (slot // own) ^ me
    pos = (rel % 8) * (npix // 8) + rel // 8
    row = pos * own + slot % own
    pix = pix_ref[...]
    column = place((pix // pxd) ^ ang, bits_of(nang)) * pxd + pix % pxd
    block = (column // 2) * (2 * rays) + (column % 2) * rays + row
    number = lax.broadcasted_iota(jnp.int32, (1, slots), 1)
    block = jnp.where(number < count_ref[0, 0], block, -1)
    rows = lax.broadcasted_iota(jnp.int32, (2 * pairs * rays, slots), 0)
    hot_ref[...] = (rows == block).astype(F32).astype(BF16)

    pack = rays // 8
    left = lax.broadcasted_iota(jnp.int32, (rays, lanes), 1) < blk
    above = lax.broadcasted_iota(jnp.int32, (pack, 8, lanes), 1) < 4

    def rows_of(sums, p, k):
        even = sums[2 * p * rays : (2 * p + 1) * rays, k * lanes : (k + 1) * lanes]
        odd = sums[(2 * p + 1) * rays : (2 * p + 2) * rays, k * lanes : (k + 1) * lanes]
        upper = jnp.where(left, even, pltpu.roll(odd, blk, 1)).reshape(pack, 8, lanes)
        lower = jnp.where(left, pltpu.roll(even, blk, 1), odd).reshape(pack, 8, lanes)
        return jnp.where(above, upper, pltpu.roll(lower, 4, 1)), jnp.where(above, pltpu.roll(upper, 4, 1), lower)

    for n in range(blk // step):
        large[n].wait()
        for g in range(step // 4):
            start = n * width + g * 2 * lanes
            high, low = split(x_ref[:, start : start + 2 * lanes])
            hot = hot_ref[...]
            sums = jnp.dot(hot, high, preferred_element_type=F32) + jnp.dot(hot, low, preferred_element_type=F32)
            at = 16 * (n * step // 4 + g)
            for p in range(pairs):
                for owner, value in enumerate(zip(rows_of(sums, p, 0), rows_of(sums, p, 1), strict=True)):
                    high, low = split(jnp.concatenate(value, axis=1))
                    out_ref[:, owner, at : at + 16, p * lanes : (p + 1) * lanes] = high
                    out_ref[:, owner, at : at + 16, (pairs + p) * lanes : (pairs + p + 1) * lanes] = low


def build(tiles, tile_ray, tile_pix, ray_slot, tile_count, dims):
    npix, nang, rays, own, pxd, blk, step = dims
    slots = tiles.shape[0]
    assert own == 4 and npix % 8 == 0 and pxd == 2
    columns = nang * pxd * blk
    shape = jax.ShapeDtypeStruct((npix // 2, 2, own * blk, 2 * columns), BF16)
    hot = jax.ShapeDtypeStruct((nang * pxd * rays, slots), BF16)
    hbm = pl.BlockSpec(memory_space=pltpu.HBM)
    small = size_of(shape) <= 6 << 20
    grant = 58 << 20 if small else limit(tiles, shape, hot)
    return pl.pallas_call(
        functools.partial(build_kernel, dims),
        in_specs=[hbm] * 5,
        out_specs=VMEM,
        out_shape=pltpu.VMEM(shape.shape, BF16) if small else shape,
        scratch_shapes=[
            pltpu.VMEM(tiles.shape, F32),
            pltpu.VMEM(tile_ray.shape, jnp.int32),
            pltpu.VMEM(tile_pix.shape, jnp.int32),
            pltpu.SMEM(ray_slot.shape, jnp.int32),
            pltpu.SMEM(tile_count.shape, jnp.int32),
            pltpu.VMEM(hot.shape, BF16),
            pltpu.SemaphoreType.DMA((4,)),
            pltpu.SemaphoreType.DMA((blk // step,)),
        ],
        compiler_params=pltpu.CompilerParams(vmem_limit_bytes=grant),
        cost_estimate=pl.CostEstimate(
            flops=4 * nang * pxd * rays * slots * blk * blk, bytes_accessed=tiles.size * 4 + 4 * rays * blk * columns, transcendentals=0
        ),
        name="build",
    )(tiles, tile_ray, tile_pix, ray_slot, tile_count).reshape(rays * blk, 2 * columns)


def loop(count, body):
    if count <= 16:
        for k in range(count):
            body(k)
    else:
        lax.fori_loop(0, count, lambda k, c: (body(k), c)[1], 0)


NT = (((1,), (1,)), ((), ()))


def project(lhs_ref, dense_ref, out_ref, start):
    pieces, tall, half = out_ref.shape
    s = (tall - EXTRA) // 2
    piece = 2 * half

    def body(k):
        rows = pl.ds(start + k * piece, piece)
        r = lax.dot_general(lhs_ref[...], dense_ref[rows, :], NT, preferred_element_type=F32)
        for h in range(2):
            part = r[:, h * half : (h + 1) * half]
            out_ref[k, h * s : (h + 1) * s, :] = part[:s] + part[s : 2 * s]
            out_ref[k, 2 * s + h : 2 * s + EXTRA, :] = part[2 * s : 2 * s + EXTRA - h]

    loop(pieces, body)


def forward_first_kernel(parts, groups, *refs):
    images, (dense_ref, *outs, lhs_ref) = refs[: len(parts)], refs[len(parts) :]
    columns = lhs_ref.shape[1] // 2
    for place_of, image_ref in zip(parts, images, strict=True):
        width, s = image_ref.shape
        high, low = split(image_ref[...].T)
        for at in (place_of * width, columns + place_of * width):
            lhs_ref[:s, at : at + width] = high
            lhs_ref[s : 2 * s, at : at + width] = low
    lhs_ref[2 * s :, :] = jnp.ones((2 * EXTRA, lhs_ref.shape[1]), BF16)
    for g, out_ref in zip(groups, outs, strict=True):
        project(lhs_ref, dense_ref, out_ref, g * (dense_ref.shape[0] // 8))


def forward_rest_kernel(groups, lhs_ref, dense_ref, *outs):
    for g, out_ref in zip(groups, outs, strict=True):
        project(lhs_ref, dense_ref, out_ref, g * (dense_ref.shape[0] // 8))


def forward(images, parts, dense, piece, first, rest):
    s = images[0].shape[1]
    rows, columns = dense.shape
    out = jax.ShapeDtypeStruct((rows // piece // 8, 2 * s + EXTRA, piece // 2), F32)
    lhs = jax.ShapeDtypeStruct((2 * s + 2 * EXTRA, columns), BF16)
    params = pltpu.CompilerParams(vmem_limit_bytes=limit(dense, lhs, *images, *[out] * len(rest)))

    def cost(groups):
        return pl.CostEstimate(
            flops=len(groups) * rows * columns * s // 2, bytes_accessed=len(groups) * rows * columns // 4, transcendentals=0
        )

    *early, lhs = pl.pallas_call(
        functools.partial(forward_first_kernel, parts, first),
        in_specs=[VMEM] * (1 + len(images)),
        out_specs=[VMEM] * (len(first) + 1),
        out_shape=[out] * len(first) + [lhs],
        cost_estimate=cost(first),
        compiler_params=params,
        name="forward_first",
    )(*images, dense)
    late = pl.pallas_call(
        functools.partial(forward_rest_kernel, rest),
        in_specs=[VMEM] * 2,
        out_specs=[VMEM] * len(rest),
        out_shape=[out] * len(rest),
        cost_estimate=cost(rest),
        compiler_params=params,
        name="forward_rest",
    )(lhs, dense)
    return dict(zip([*first, *rest], [*early, *late], strict=True))


def spread(resid_ref, dense_ref, start, total):
    pieces, piece, s = resid_ref.shape[0], 2 * resid_ref.shape[2], resid_ref.shape[1] // 2
    columns = total.shape[1]
    ones = jnp.ones((2 * EXTRA, piece), BF16)

    def body(k):
        resid = jnp.concatenate([resid_ref[k, :s], resid_ref[k, s:]], axis=1)
        lhs = jnp.concatenate([*split(resid), ones], axis=0)
        rows = pl.ds(start + k * piece, piece)
        both = jnp.concatenate([dense_ref[rows, :columns], dense_ref[rows, columns:]], axis=0)
        total[...] += jnp.dot(jnp.concatenate([lhs, lhs], axis=1), both, preferred_element_type=F32)

    loop(pieces, body)


def backward_kernel(groups, first, last, *refs):
    resids, (dense_ref, *rest) = refs[: len(groups)], refs[len(groups) :]
    total = rest[-1]
    total[...] = jnp.zeros_like(total) if first else rest[0][...]
    for g, resid_ref in zip(groups, resids, strict=True):
        spread(resid_ref, dense_ref, g * (dense_ref.shape[0] // 8), total)
    if last:
        kept_ref, sent_ref = rest[-3:-1]
        pieces, tall, width = kept_ref.shape
        s = tall - EXTRA
        for p in range(2 * pieces):
            out_ref, k = (kept_ref, p) if p < pieces else (sent_ref, p - pieces)
            part = total[:, p * width : (p + 1) * width]
            out_ref[k, :s, :] = part[:s] + part[s : 2 * s]
            out_ref[k, s:, :] = part[2 * s : 2 * s + EXTRA]


def backward(resids, dense, parts, before, last):
    s = next(iter(resids.values())).shape[1] // 2
    rows, columns = dense.shape[0], dense.shape[1] // 2
    total = jax.ShapeDtypeStruct((2 * s + 2 * EXTRA, columns), F32)
    out = jax.ShapeDtypeStruct((parts // 2, s + EXTRA, columns // parts), F32)
    operands = [*resids.values(), dense] + ([] if before is None else [before])
    return pl.pallas_call(
        functools.partial(backward_kernel, list(resids), before is None, last),
        in_specs=[VMEM] * len(operands),
        out_specs=[VMEM] * 2 if last else VMEM,
        out_shape=[out, out] if last else total,
        scratch_shapes=[pltpu.VMEM(total.shape, F32)] if last else [],
        cost_estimate=pl.CostEstimate(
            flops=len(resids) * rows * columns * s, bytes_accessed=len(resids) * rows * columns // 2, transcendentals=0
        ),
        compiler_params=pltpu.CompilerParams(vmem_limit_bytes=limit(total, total, *operands)),
        name="backward",
    )(*operands)


def prepare_kernel(own, measured_ref, out_ref, rows_ref):
    blk, half = measured_ref.shape[0] // own, out_ref.shape[1]
    s = out_ref.shape[0] // 2
    for r in range(own):
        rows_ref[pl.ds(r, blk, stride=own), :] = measured_ref[r * blk : (r + 1) * blk, :]
    for h in range(2):
        out_ref[h * s : (h + 1) * s, :] = rows_ref[h * half : (h + 1) * half, :].T


def restore_kernel(own, resid_ref, out_ref, rows_ref):
    blk, half = out_ref.shape[0] // own, resid_ref.shape[1]
    s = resid_ref.shape[0] // 2
    for h in range(2):
        rows_ref[h * half : (h + 1) * half, :] = resid_ref[h * s : (h + 1) * s, :].T
    for r in range(own):
        out_ref[r * blk : (r + 1) * blk, :] = rows_ref[pl.ds(r, blk, stride=own), :]


def turn(kernel, own, x, out, rows):
    return pl.pallas_call(
        functools.partial(kernel, own),
        in_specs=[VMEM],
        out_specs=VMEM,
        out_shape=jax.ShapeDtypeStruct(out, F32),
        scratch_shapes=[pltpu.VMEM(rows, F32)],
        compiler_params=pltpu.CompilerParams(vmem_limit_bytes=limit(x, x)),
        cost_estimate=pl.CostEstimate(flops=x.size, bytes_accessed=8 * x.size, transcendentals=0),
    )(x)


def swap(x, axis, mask):
    return lax.ppermute(x, axis, [(i, i ^ mask) for i in range(lax.axis_size(axis))])


def shards(tiles, tile_ray, tile_pix, tile_count, ray_slot, image, measured):
    npix, nang = lax.axis_size("pix"), lax.axis_size("ang")
    rays, slots = ray_slot.shape[1], tiles.shape[2]
    own = rays // npix
    blk = measured.shape[1] // own
    s = image.shape[1]
    pxd = image.shape[0] // blk
    dims = (npix, nang, rays, own, pxd, blk, 16)
    piece = own * blk
    more = bits_of(npix)[3:]

    images = [image] + [swap(image, "ang", r) for r in range(1, nang)]
    dense = build(tiles.reshape(slots, blk * blk), tile_ray[0], tile_pix[0], ray_slot, tile_count, dims)
    parts = [int(place(np.int32(r), bits_of(nang))) for r in range(nang)]

    proj = forward(images, parts, dense, piece, [7, 5, 6], [1, 2, 3, 4, 0])
    far = [swap(proj[4 + d], "pix", d) for d in (2, 1, 3)]
    crossing = swap(proj[4] + far[0] + far[1] + far[2], "pix", 4)
    near = [swap(proj[d], "pix", d) for d in (1, 2, 3)]
    total = proj[0] + near[0] + near[1] + near[2] + crossing
    for bit in reversed(more):
        m = total.shape[0] // 2
        total = total[:m] + swap(total[m:], "pix", 1 << bit)
    total = total[0]
    straight, turned = (piece, s), (2 * s, piece // 2)
    wanted = turn(prepare_kernel, own, measured[0], turned, straight)
    resid = jnp.concatenate(
        [(wanted[h * s : (h + 1) * s] - total[h * s : (h + 1) * s]) / total[2 * s + h][None] for h in range(2)]
    )
    resid_own = turn(restore_kernel, own, resid, straight, straight)[None]

    held = resid[None]
    for bit in more:
        held = jnp.concatenate([held, swap(held, "pix", 1 << bit)])
    got = {0: held, 4: swap(held, "pix", 4)}
    for d in (1, 2, 3):
        got[d] = swap(held, "pix", d)
    for d in (2, 1, 3):
        got[4 + d] = swap(got[4], "pix", d)
    turns = [(0, 1, 2, 3), (4, 7), (5,), (6,)]
    back = None
    for k, groups in enumerate(turns):
        back = backward({g: got[g] for g in groups}, dense, nang, back, k == len(turns) - 1)
    kept, sent = back
    for bit in bits_of(nang):
        arrived = swap(sent, "ang", 1 << bit)
        m = kept.shape[0] // 2
        kept, sent = (kept[:m] + arrived[:m], kept[m:] + arrived[m:]) if m else (kept + arrived, None)
    back = kept[0]
    new_image = image + RELAX * (back[:s] / back[s : s + 1]).T
    return new_image, resid_own


def solution(mesh):
    in_specs = (
        P("pix", "ang", None, None),
        P("pix", "ang", None),
        P("pix", "ang", None),
        P("pix", "ang"),
        P("ang", None),
        P(("pix", "ang"), None),
        P("ang", "pix", None),
    )
    out_specs = (P(("pix", "ang"), None), P("ang", "pix", None))
    return jax.shard_map(shards, mesh=mesh, in_specs=in_specs, out_specs=out_specs, check_vma=False)
```

```python
import functools

import jax
import jax.numpy as jnp
import numpy as np
from jax import lax
from jax.experimental import pallas as pl
from jax.experimental.pallas import tpu as pltpu
from jax.sharding import PartitionSpec as P


RELAX = 0.9
F32 = jnp.float32
BF16 = jnp.bfloat16
EXTRA = 8


def split(x):
    high = x.astype(BF16)
    return high, (x - high.astype(F32)).astype(BF16)


def place(rel, order):
    pos = rel * 0
    for bit in order:
        pos = pos * 2 + ((rel >> bit) & 1)
    return pos


def bits_of(size):
    return list(range(size.bit_length() - 1))


def size_of(*shapes):
    total = 0
    for x in shapes:
        count = 1
        for d in x.shape:
            count *= d
        total += count * jnp.dtype(x.dtype).itemsize
    return total


def limit(*shapes):
    return min(size_of(*shapes) + (6 << 20), 60 << 20)


VMEM = pl.BlockSpec(memory_space=pltpu.VMEM)


def build_kernel(dims, x_hbm, ray_hbm, pix_hbm, slots_hbm, count_hbm, out_ref, *scratch):
    npix, nang, rays, own, pxd, blk, step = dims
    x_ref, ray_ref, pix_ref, slots_ref, count_ref, hot_ref, small_sem, x_sem = scratch
    slots = ray_ref.shape[1]
    pairs = nang * pxd // 2
    lanes = 2 * blk
    small = [
        pltpu.make_async_copy(source, target, small_sem.at[k])
        for k, (source, target) in enumerate(
            ((ray_hbm, ray_ref), (pix_hbm, pix_ref), (slots_hbm, slots_ref), (count_hbm, count_ref))
        )
    ]
    width = step * blk
    large = [
        pltpu.make_async_copy(x_hbm.at[:, pl.ds(k * width, width)], x_ref.at[:, pl.ds(k * width, width)], x_sem.at[k])
        for k in range(blk // step)
    ]
    for copy in small + large:
        copy.start()
    for copy in small:
        copy.wait()

    me, ang = lax.axis_index("pix"), lax.axis_index("ang")
    ray = ray_ref[...]
    slot = jnp.zeros_like(ray)
    for r in range(rays):
        slot = jnp.where(ray == r, slots_ref[0, r], slot)
    rel = (slot // own) ^ me
    pos = (rel % 8) * (npix // 8) + rel // 8
    row = pos * own + slot % own
    pix = pix_ref[...]
    column = place((pix // pxd) ^ ang, bits_of(nang)) * pxd + pix % pxd
    block = (column // 2) * (2 * rays) + (column % 2) * rays + row
    number = lax.broadcasted_iota(jnp.int32, (1, slots), 1)
    block = jnp.where(number < count_ref[0, 0], block, -1)
    rows = lax.broadcasted_iota(jnp.int32, (2 * pairs * rays, slots), 0)
    hot_ref[...] = (rows == block).astype(F32).astype(BF16)

    pack = rays // 8
    left = lax.broadcasted_iota(jnp.int32, (rays, lanes), 1) < blk
    above = lax.broadcasted_iota(jnp.int32, (pack, 8, lanes), 1) < 4

    def rows_of(sums, p, k):
        even = sums[2 * p * rays : (2 * p + 1) * rays, k * lanes : (k + 1) * lanes]
        odd = sums[(2 * p + 1) * rays : (2 * p + 2) * rays, k * lanes : (k + 1) * lanes]
        upper = jnp.where(left, even, pltpu.roll(odd, blk, 1)).reshape(pack, 8, lanes)
        lower = jnp.where(left, pltpu.roll(even, blk, 1), odd).reshape(pack, 8, lanes)
        return jnp.where(above, upper, pltpu.roll(lower, 4, 1)), jnp.where(above, pltpu.roll(upper, 4, 1), lower)

    for n in range(blk // step):
        large[n].wait()
        for g in range(step // 4):
            start = n * width + g * 2 * lanes
            high, low = split(x_ref[:, start : start + 2 * lanes])
            hot = hot_ref[...]
            sums = jnp.dot(hot, high, preferred_element_type=F32) + jnp.dot(hot, low, preferred_element_type=F32)
            at = 16 * (n * step // 4 + g)
            for p in range(pairs):
                for owner, value in enumerate(zip(rows_of(sums, p, 0), rows_of(sums, p, 1), strict=True)):
                    high, low = split(jnp.concatenate(value, axis=1))
                    out_ref[:, owner, at : at + 16, p * lanes : (p + 1) * lanes] = high
                    out_ref[:, owner, at : at + 16, (pairs + p) * lanes : (pairs + p + 1) * lanes] = low


def build(tiles, tile_ray, tile_pix, ray_slot, tile_count, dims):
    npix, nang, rays, own, pxd, blk, step = dims
    slots = tiles.shape[0]
    assert own == 4 and npix % 8 == 0 and pxd == 2
    columns = nang * pxd * blk
    shape = jax.ShapeDtypeStruct((npix // 2, 2, own * blk, 2 * columns), BF16)
    hot = jax.ShapeDtypeStruct((nang * pxd * rays, slots), BF16)
    hbm = pl.BlockSpec(memory_space=pltpu.HBM)
    small = size_of(shape) <= 6 << 20
    grant = 58 << 20 if small else limit(tiles, shape, hot)
    return pl.pallas_call(
        functools.partial(build_kernel, dims),
        in_specs=[hbm] * 5,
        out_specs=VMEM,
        out_shape=pltpu.VMEM(shape.shape, BF16) if small else shape,
        scratch_shapes=[
            pltpu.VMEM(tiles.shape, F32),
            pltpu.VMEM(tile_ray.shape, jnp.int32),
            pltpu.VMEM(tile_pix.shape, jnp.int32),
            pltpu.SMEM(ray_slot.shape, jnp.int32),
            pltpu.SMEM(tile_count.shape, jnp.int32),
            pltpu.VMEM(hot.shape, BF16),
            pltpu.SemaphoreType.DMA((4,)),
            pltpu.SemaphoreType.DMA((blk // step,)),
        ],
        compiler_params=pltpu.CompilerParams(vmem_limit_bytes=grant),
        cost_estimate=pl.CostEstimate(
            flops=4 * nang * pxd * rays * slots * blk * blk, bytes_accessed=tiles.size * 4 + 4 * rays * blk * columns, transcendentals=0
        ),
        name="build",
    )(tiles, tile_ray, tile_pix, ray_slot, tile_count).reshape(rays * blk, 2 * columns)


def loop(count, body):
    if count <= 16:
        for k in range(count):
            body(k)
    else:
        lax.fori_loop(0, count, lambda k, c: (body(k), c)[1], 0)


NT = (((1,), (1,)), ((), ()))


def project(lhs_ref, dense_ref, out_ref, start):
    pieces, tall, half = out_ref.shape
    s = (tall - EXTRA) // 2
    piece = 2 * half

    def body(k):
        rows = pl.ds(start + k * piece, piece)
        r = lax.dot_general(lhs_ref[...], dense_ref[rows, :], NT, preferred_element_type=F32)
        for h in range(2):
            part = r[:, h * half : (h + 1) * half]
            out_ref[k, h * s : (h + 1) * s, :] = part[:s] + part[s : 2 * s]
            out_ref[k, 2 * s + h : 2 * s + EXTRA, :] = part[2 * s : 2 * s + EXTRA - h]

    loop(pieces, body)


def forward_first_kernel(parts, groups, *refs):
    images, (dense_ref, *outs, lhs_ref) = refs[: len(parts)], refs[len(parts) :]
    columns = lhs_ref.shape[1] // 2
    for place_of, image_ref in zip(parts, images, strict=True):
        width, s = image_ref.shape
        high, low = split(image_ref[...].T)
        for at in (place_of * width, columns + place_of * width):
            lhs_ref[:s, at : at + width] = high
            lhs_ref[s : 2 * s, at : at + width] = low
    lhs_ref[2 * s :, :] = jnp.ones((2 * EXTRA, lhs_ref.shape[1]), BF16)
    for g, out_ref in zip(groups, outs, strict=True):
        project(lhs_ref, dense_ref, out_ref, g * (dense_ref.shape[0] // 8))


def forward_rest_kernel(groups, lhs_ref, dense_ref, *outs):
    for g, out_ref in zip(groups, outs, strict=True):
        project(lhs_ref, dense_ref, out_ref, g * (dense_ref.shape[0] // 8))


def forward(images, parts, dense, piece, first, rest):
    s = images[0].shape[1]
    rows, columns = dense.shape
    out = jax.ShapeDtypeStruct((rows // piece // 8, 2 * s + EXTRA, piece // 2), F32)
    lhs = jax.ShapeDtypeStruct((2 * s + 2 * EXTRA, columns), BF16)
    params = pltpu.CompilerParams(vmem_limit_bytes=limit(dense, lhs, *images, *[out] * len(rest)))

    def cost(groups):
        return pl.CostEstimate(
            flops=len(groups) * rows * columns * s // 2, bytes_accessed=len(groups) * rows * columns // 4, transcendentals=0
        )

    *early, lhs = pl.pallas_call(
        functools.partial(forward_first_kernel, parts, first),
        in_specs=[VMEM] * (1 + len(images)),
        out_specs=[VMEM] * (len(first) + 1),
        out_shape=[out] * len(first) + [lhs],
        cost_estimate=cost(first),
        compiler_params=params,
        name="forward_first",
    )(*images, dense)
    late = pl.pallas_call(
        functools.partial(forward_rest_kernel, rest),
        in_specs=[VMEM] * 2,
        out_specs=[VMEM] * len(rest),
        out_shape=[out] * len(rest),
        cost_estimate=cost(rest),
        compiler_params=params,
        name="forward_rest",
    )(lhs, dense)
    return dict(zip([*first, *rest], [*early, *late], strict=True))


def spread(resid_ref, dense_ref, start, total):
    pieces, piece, s = resid_ref.shape[0], 2 * resid_ref.shape[2], resid_ref.shape[1] // 2
    columns = total.shape[1]
    ones = jnp.ones((2 * EXTRA, piece), BF16)

    def body(k):
        resid = jnp.concatenate([resid_ref[k, :s], resid_ref[k, s:]], axis=1)
        lhs = jnp.concatenate([*split(resid), ones], axis=0)
        rows = pl.ds(start + k * piece, piece)
        both = jnp.concatenate([dense_ref[rows, :columns], dense_ref[rows, columns:]], axis=0)
        total[...] += jnp.dot(jnp.concatenate([lhs, lhs], axis=1), both, preferred_element_type=F32)

    loop(pieces, body)


def backward_kernel(groups, first, last, *refs):
    resids, (dense_ref, *rest) = refs[: len(groups)], refs[len(groups) :]
    total = rest[-1]
    total[...] = jnp.zeros_like(total) if first else rest[0][...]
    for g, resid_ref in zip(groups, resids, strict=True):
        spread(resid_ref, dense_ref, g * (dense_ref.shape[0] // 8), total)
    if last:
        kept_ref, sent_ref = rest[-3:-1]
        pieces, tall, width = kept_ref.shape
        s = tall - EXTRA
        for p in range(2 * pieces):
            out_ref, k = (kept_ref, p) if p < pieces else (sent_ref, p - pieces)
            part = total[:, p * width : (p + 1) * width]
            out_ref[k, :s, :] = part[:s] + part[s : 2 * s]
            out_ref[k, s:, :] = part[2 * s : 2 * s + EXTRA]


def backward(resids, dense, parts, before, last):
    s = next(iter(resids.values())).shape[1] // 2
    rows, columns = dense.shape[0], dense.shape[1] // 2
    total = jax.ShapeDtypeStruct((2 * s + 2 * EXTRA, columns), F32)
    out = jax.ShapeDtypeStruct((parts // 2, s + EXTRA, columns // parts), F32)
    operands = [*resids.values(), dense] + ([] if before is None else [before])
    return pl.pallas_call(
        functools.partial(backward_kernel, list(resids), before is None, last),
        in_specs=[VMEM] * len(operands),
        out_specs=[VMEM] * 2 if last else VMEM,
        out_shape=[out, out] if last else total,
        scratch_shapes=[pltpu.VMEM(total.shape, F32)] if last else [],
        cost_estimate=pl.CostEstimate(
            flops=len(resids) * rows * columns * s, bytes_accessed=len(resids) * rows * columns // 2, transcendentals=0
        ),
        compiler_params=pltpu.CompilerParams(vmem_limit_bytes=limit(total, total, *operands)),
        name="backward",
    )(*operands)


def finish_kernel(group, side, resid_ref, dense_ref, before_ref, out_ref, total_ref):
    parts, tall, width = out_ref.shape
    s, piece, columns = tall - EXTRA, 2 * resid_ref.shape[2], before_ref.shape[1]
    ones = jnp.ones((2 * EXTRA, piece), BF16)
    span = parts * width
    total_ref[...] = before_ref[:, side * span : (side + 1) * span]

    def body(k):
        resid = jnp.concatenate([resid_ref[k, :s], resid_ref[k, s:]], axis=1)
        lhs = jnp.concatenate([*split(resid), ones], axis=0)
        rows = pl.ds(group * (dense_ref.shape[0] // 8) + k * piece, piece)
        both = [dense_ref[rows, at + side * span : at + (side + 1) * span] for at in (0, columns)]
        total_ref[...] += jnp.dot(
            jnp.concatenate([lhs, lhs], axis=1), jnp.concatenate(both, axis=0), preferred_element_type=F32
        )

    loop(resid_ref.shape[0], body)
    for p in range(parts):
        part = total_ref[:, p * width : (p + 1) * width]
        out_ref[p, :s, :] = part[:s] + part[s : 2 * s]
        out_ref[p, s:, :] = part[2 * s : 2 * s + EXTRA]


def finish(resid, group, dense, parts, before, side):
    tall, columns = before.shape
    s = resid.shape[1] // 2
    return pl.pallas_call(
        functools.partial(finish_kernel, group, side),
        in_specs=[VMEM] * 3,
        out_specs=VMEM,
        out_shape=jax.ShapeDtypeStruct((parts // 2, s + EXTRA, columns // parts), F32),
        scratch_shapes=[pltpu.VMEM((tall, columns // 2), F32)],
        cost_estimate=pl.CostEstimate(flops=dense.size * s // 4, bytes_accessed=dense.size // 4, transcendentals=0),
        compiler_params=pltpu.CompilerParams(vmem_limit_bytes=limit(before, before, resid, dense)),
        name="finish",
    )(resid, dense, before)


def prepare_kernel(own, measured_ref, out_ref, rows_ref):
    blk, half = measured_ref.shape[0] // own, out_ref.shape[1]
    s = out_ref.shape[0] // 2
    for r in range(own):
        rows_ref[pl.ds(r, blk, stride=own), :] = measured_ref[r * blk : (r + 1) * blk, :]
    for h in range(2):
        out_ref[h * s : (h + 1) * s, :] = rows_ref[h * half : (h + 1) * half, :].T


def restore_kernel(own, resid_ref, out_ref, rows_ref):
    blk, half = out_ref.shape[0] // own, resid_ref.shape[1]
    s = resid_ref.shape[0] // 2
    for h in range(2):
        rows_ref[h * half : (h + 1) * half, :] = resid_ref[h * s : (h + 1) * s, :].T
    for r in range(own):
        out_ref[r * blk : (r + 1) * blk, :] = rows_ref[pl.ds(r, blk, stride=own), :]


def turn(kernel, own, x, out, rows):
    return pl.pallas_call(
        functools.partial(kernel, own),
        in_specs=[VMEM],
        out_specs=VMEM,
        out_shape=jax.ShapeDtypeStruct(out, F32),
        scratch_shapes=[pltpu.VMEM(rows, F32)],
        compiler_params=pltpu.CompilerParams(vmem_limit_bytes=limit(x, x)),
        cost_estimate=pl.CostEstimate(flops=x.size, bytes_accessed=8 * x.size, transcendentals=0),
    )(x)


def swap(x, axis, mask):
    return lax.ppermute(x, axis, [(i, i ^ mask) for i in range(lax.axis_size(axis))])


def shards(tiles, tile_ray, tile_pix, tile_count, ray_slot, image, measured):
    npix, nang = lax.axis_size("pix"), lax.axis_size("ang")
    rays, slots = ray_slot.shape[1], tiles.shape[2]
    own = rays // npix
    blk = measured.shape[1] // own
    s = image.shape[1]
    pxd = image.shape[0] // blk
    dims = (npix, nang, rays, own, pxd, blk, 16)
    piece = own * blk
    more = bits_of(npix)[3:]

    images = [image] + [swap(image, "ang", r) for r in range(1, nang)]
    dense = build(tiles.reshape(slots, blk * blk), tile_ray[0], tile_pix[0], ray_slot, tile_count, dims)
    parts = [int(place(np.int32(r), bits_of(nang))) for r in range(nang)]

    proj = forward(images, parts, dense, piece, [7, 5, 6], [1, 2, 3, 4, 0])
    far = [swap(proj[4 + d], "pix", d) for d in (2, 1, 3)]
    crossing = swap(proj[4] + far[0] + far[1] + far[2], "pix", 4)
    near = [swap(proj[d], "pix", d) for d in (1, 2, 3)]
    total = proj[0] + near[0] + near[1] + near[2] + crossing
    for bit in reversed(more):
        m = total.shape[0] // 2
        total = total[:m] + swap(total[m:], "pix", 1 << bit)
    total = total[0]
    straight, turned = (piece, s), (2 * s, piece // 2)
    wanted = turn(prepare_kernel, own, measured[0], turned, straight)
    resid = jnp.concatenate(
        [(wanted[h * s : (h + 1) * s] - total[h * s : (h + 1) * s]) / total[2 * s + h][None] for h in range(2)]
    )
    resid_own = turn(restore_kernel, own, resid, straight, straight)[None]

    held = resid[None]
    for bit in more:
        held = jnp.concatenate([held, swap(held, "pix", 1 << bit)])
    got = {0: held, 4: swap(held, "pix", 4)}
    for d in (1, 2, 3):
        got[d] = swap(held, "pix", d)
    for d in (2, 1, 3):
        got[4 + d] = swap(got[4], "pix", d)
    back = None
    for groups in ((0, 1, 2, 3), (4, 7), (5,)):
        back = backward({g: got[g] for g in groups}, dense, nang, back, False)
    sent = finish(got[6], 6, dense, nang, back, 1)
    kept = finish(got[6], 6, dense, nang, back, 0)
    for bit in bits_of(nang):
        arrived = swap(sent, "ang", 1 << bit)
        m = kept.shape[0] // 2
        kept, sent = (kept[:m] + arrived[:m], kept[m:] + arrived[m:]) if m else (kept + arrived, None)
    back = kept[0]
    new_image = image + RELAX * (back[:s] / back[s : s + 1]).T
    return new_image, resid_own


def solution(mesh):
    in_specs = (
        P("pix", "ang", None, None),
        P("pix", "ang", None),
        P("pix", "ang", None),
        P("pix", "ang"),
        P("ang", None),
        P(("pix", "ang"), None),
        P("ang", "pix", None),
    )
    out_specs = (P(("pix", "ang"), None), P("ang", "pix", None))
    return jax.shard_map(shards, mesh=mesh, in_specs=in_specs, out_specs=out_specs, check_vma=False)
```
